32 devices in a mesh: dp: 8 (over z, y), tensor: 4 (over x, core).
Axes of the slice: x: 2, y: 2, z: 4, core: 2. Of those that a mesh axis runs over, the one named last changes fastest.
Arguments:
- tokens: bfloat16 [256, 8192], P('dp'), may hold values from -6 to 6
- output_gradient: bfloat16 [256, 8192], P('dp'), may hold values from -6 to 6
- gate_up_weight: bfloat16 [8192, 2, 26624], P('dp', None, 'tensor'), may hold values from -0.0625 to 0.0625
- down_weight: bfloat16 [26624, 8192], P('tensor', 'dp'), may hold values from -0.0390625 to 0.0390625
- adapter_input_factor: bfloat16 [512, 16, 8192], P('tensor', None, 'dp'), may hold values from -0.0625 to 0.0625
- adapter_output_factor: bfloat16 [512, 16, 26624], P('dp', None, 'tensor'), may hold values from -1.5 to 1.5
- request_token_rows: int32 [8, 4], replicated, may hold values from 1 to 16, 32 in all within a row
- request_adapter: int32 [8, 4], replicated, may hold values from 0 to 511
- adapter_table_row: int32 [512], replicated, may hold values from 0 to 511, each once
Outputs:
- layer_output: bfloat16 [256, 8192], P('tensor', 'dp')
- input_gradient: bfloat16 [256, 8192], P('tensor', 'dp')
- adapter_input_gradient: bfloat16 [512, 16, 8192], P('tensor', None, 'dp')
- adapter_output_gradient: bfloat16 [512, 16, 26624], P('dp', None, 'tensor')
The draws below stay inside these ranges and needn't reach their ends.
Inputs may be any that keep to these rules, and one draw needn't show every extreme that they name: Each row of request_token_rows sums to 32, and its largest entry is 16. `adapter_table_row`: every table row from 0 to 511 appears once.
All inputs are finite; a program needn't handle non-finite values.
Results may differ from the reference program's by a relative error of at most 0.0059.
Values may be sent and summed in bfloat16 or wider, within the bound.
A program may use at most 192 MiB of HBM per device.

```python
import math
import jax
import jax.numpy as jnp
import numpy as np
from jax import lax

MODEL_WIDTH = 8192
HIDDEN_UNITS = 26624
ADAPTER_COUNT = 512
ADAPTER_RANK = 16
REQ_DEV = 4
TOK_DEV = 32
LEN_MAX = 16
TOKENS = 256
N_DP = 8


def set_ends(drawn, key, least, top_value):
    longest = drawn.shape.index(max(drawn.shape))
    spots = []
    for shift in (0, 1):
        where = [jax.random.randint(jax.random.fold_in(key, axis), (), 0, length) for axis, length in enumerate(drawn.shape)]
        where[longest] = (where[longest] + shift) % drawn.shape[longest]
        spots.append(tuple(where))
    return drawn.at[spots[0]].set(least).at[spots[1]].set(top_value)


def block_levels(own_key, dims, cuts, smallest, top_value):
    def one(dim, shards_of):
        draws = jax.random.uniform(jax.random.fold_in(jax.random.fold_in(own_key, 6), dim), (shards_of,), jnp.float32, smallest / len(cuts), top_value / len(cuts))
        return jnp.repeat(jnp.exp(draws), dims[dim] // shards_of).reshape((-1,) + (1,) * (len(dims) - dim - 1))

    loudness = one(*cuts[0])
    for cut in cuts[1:]:
        loudness = loudness * one(*cut)
    return loudness


def length_profile(count, total, bound, lean):
    portions = [(1 << 20) // math.isqrt(standing ** lean) + 1 for standing in range(2, count + 1)]
    rest, holding = total - bound - (count - 1), [1] * (count - 1)
    while rest > 0:
        movable = [i for i in range(count - 1) if holding[i] < bound]
        whole, left = sum([portions[i] for i in movable]), rest
        for i in movable:
            more = min(bound - holding[i], max(1, left * portions[i] // whole), rest)
            holding[i] = holding[i] + more
            rest = rest - more
    return np.array([bound] + holding)


def uneven(rng, amount, total, limit, slope):
    if amount == 2:
        one = jax.random.randint(rng, (), max(1, total - limit), min(limit, total - 1) + 1)
        return jnp.stack([one, total - one])
    tallies = jnp.asarray(length_profile(amount, total, limit, slope), jnp.int32)
    couples = (amount - 1) // 2
    giver, taker = tallies[1:1 + 2 * couples:2], tallies[2:2 + 2 * couples:2]
    margin = jnp.minimum(giver - 1, limit - taker)
    passed = jax.random.randint(jax.random.fold_in(rng, 1), (couples,), 0, 1 << 20) % (margin + 1)
    tallies = tallies.at[1:1 + 2 * couples:2].set(giver - passed).at[2:2 + 2 * couples:2].set(taker + passed)
    return tallies[jax.random.permutation(jax.random.fold_in(rng, 2), amount)]


def bell_draw(stream_key, dims, width, reach, cuts=(), held_as=jnp.bfloat16):
    level = block_levels(stream_key, dims, cuts, -0.22, 0.18) if cuts else 1.0
    values = jax.random.normal(stream_key, dims, jnp.float32) * width * level
    return jnp.minimum(jnp.maximum(values, -reach), reach).astype(held_as)


def setup_inputs(seed: int = 0) -> dict:
    arg_keys = jax.random.split(jax.random.key(seed), 10)
    tokens = bell_draw(arg_keys[0], (TOKENS, MODEL_WIDTH), 1.0, 6.0, ((0, 8),))
    output_gradient = bell_draw(arg_keys[1], (TOKENS, MODEL_WIDTH), 1.0, 6.0, ((0, 8),))
    gate_up_weight = bell_draw(arg_keys[2], (MODEL_WIDTH, 2, HIDDEN_UNITS), MODEL_WIDTH ** -0.5, 0.0625, ((0, 8), (2, 4)))
    down_weight = bell_draw(arg_keys[3], (HIDDEN_UNITS, MODEL_WIDTH), HIDDEN_UNITS ** -0.5, 0.0390625, ((0, 4), (1, 8)))
    adapter_input_factor = bell_draw(arg_keys[4], (ADAPTER_COUNT, ADAPTER_RANK, MODEL_WIDTH), MODEL_WIDTH ** -0.5, 0.0625, ((0, 4), (2, 8)))
    adapter_output_factor = bell_draw(arg_keys[5], (ADAPTER_COUNT, ADAPTER_RANK, HIDDEN_UNITS), ADAPTER_RANK ** -0.5, 1.5, ((0, 8), (2, 4)))
    request_token_rows = jax.vmap(lambda own: uneven(own, REQ_DEV, TOK_DEV, LEN_MAX, 2))(jax.random.split(arg_keys[6], N_DP)).reshape((N_DP, REQ_DEV)).astype(jnp.int32)
    request_adapter = set_ends(jax.random.randint(arg_keys[7], (N_DP, REQ_DEV), 0, ADAPTER_COUNT), jax.random.fold_in(arg_keys[7], 1), 0, ADAPTER_COUNT - 1).astype(jnp.int32)
    adapter_table_row = jax.random.permutation(arg_keys[8], ADAPTER_COUNT).astype(jnp.int32)
    return dict(tokens=tokens, output_gradient=output_gradient, gate_up_weight=gate_up_weight, down_weight=down_weight, adapter_input_factor=adapter_input_factor, adapter_output_factor=adapter_output_factor, request_token_rows=request_token_rows, request_adapter=request_adapter, adapter_table_row=adapter_table_row)


adapter_scale = 0.5


def row_slots(request_token_rows, request_adapter, adapter_table_row, group_rows):
    request_count = request_token_rows.shape[1]
    run_ends = jnp.cumsum(request_token_rows, axis=1).astype(jnp.int32)
    position = jnp.arange(group_rows, dtype=jnp.int32)
    request_of = jnp.sum((run_ends[:, None, :] <= position[None, :, None]).astype(jnp.int32), axis=2).astype(jnp.int32)
    request_ids = jnp.arange(request_count, dtype=jnp.int32)
    adapter_of = jnp.sum(jnp.where(request_of[:, :, None] == request_ids[None, None, :], request_adapter[:, None, :], 0), axis=2).astype(jnp.int32)
    adapter_ids = jnp.arange(adapter_table_row.shape[0], dtype=jnp.int32)
    flat_adapter = adapter_of.reshape(-1)
    return jnp.sum(jnp.where(flat_adapter[:, None] == adapter_ids[None, :], adapter_table_row[None, :], 0), axis=1).astype(jnp.int32)


def reference(tokens, output_gradient, gate_up_weight, down_weight, adapter_input_factor, adapter_output_factor, request_token_rows, request_adapter, adapter_table_row):
    groups = request_token_rows.shape[0]
    group_rows = tokens.shape[0] // groups
    slot_of = row_slots(request_token_rows, request_adapter, adapter_table_row, group_rows)
    table_row_blocks = slot_of.reshape(groups, group_rows)
    token_blocks = tokens.reshape(groups, group_rows, tokens.shape[1])

    def codes_of(block):
        token_row_block, table_row_list = block
        return jnp.einsum("ulq,uq->ul", adapter_input_factor[table_row_list].astype(jnp.float32), token_row_block.astype(jnp.float32))

    codes_total_sum = lax.map(codes_of, (token_blocks, table_row_blocks)).reshape(tokens.shape[0], ADAPTER_RANK)
    code_low = codes_total_sum.astype(jnp.bfloat16)
    code_blocks = code_low.reshape(groups, group_rows, ADAPTER_RANK)

    def lift_of(block):
        codes_per_row, table_row_list = block
        return jnp.einsum("uz,uzv->uv", codes_per_row.astype(jnp.float32), adapter_output_factor[table_row_list].astype(jnp.float32))

    raised_codes = lax.map(lift_of, (code_blocks, table_row_blocks)).reshape(tokens.shape[0], HIDDEN_UNITS)
    gate_pre = jnp.dot(tokens, gate_up_weight[:, 0, :], preferred_element_type=jnp.float32)
    up_activation = jnp.dot(tokens, gate_up_weight[:, 1, :], preferred_element_type=jnp.float32) + adapter_scale * raised_codes
    sigmoid_gate = jax.nn.sigmoid(gate_pre)
    hidden = (gate_pre * sigmoid_gate * up_activation).astype(jnp.bfloat16)
    layer_output = jnp.dot(hidden, down_weight, preferred_element_type=jnp.float32).astype(jnp.bfloat16)
    hidden_grad = jnp.dot(output_gradient, down_weight.T, preferred_element_type=jnp.float32)
    gate_grad = (hidden_grad * up_activation * sigmoid_gate * (1.0 + gate_pre * (1.0 - sigmoid_gate))).astype(jnp.bfloat16)
    up_grad = (hidden_grad * gate_pre * sigmoid_gate).astype(jnp.bfloat16)
    up_weight_blocks = up_grad.reshape(groups, group_rows, HIDDEN_UNITS)

    def backward_codes(block):
        up_weight_rows, table_row_list = block
        return jnp.einsum("lb,lhb->lh", up_weight_rows.astype(jnp.float32), adapter_output_factor[table_row_list].astype(jnp.float32))

    codes_gradient = adapter_scale * lax.map(backward_codes, (up_weight_blocks, table_row_blocks)).reshape(tokens.shape[0], ADAPTER_RANK)
    code_grad_low = codes_gradient.astype(jnp.bfloat16)
    gradient_blocks = code_grad_low.reshape(groups, group_rows, ADAPTER_RANK)

    def backward_input(block):
        gradient_rows, table_row_list = block
        return jnp.einsum("hl,hle->he", gradient_rows.astype(jnp.float32), adapter_input_factor[table_row_list].astype(jnp.float32))

    adapter_input_rows = lax.map(backward_input, (gradient_blocks, table_row_blocks)).reshape(tokens.shape[0], MODEL_WIDTH)
    input_gradient = (jnp.dot(gate_grad, gate_up_weight[:, 0, :].T, preferred_element_type=jnp.float32)
               + jnp.dot(up_grad, gate_up_weight[:, 1, :].T, preferred_element_type=jnp.float32)
               + adapter_input_rows).astype(jnp.bfloat16)

    def add_grads(running_totals, block):
        input_total, output_total = running_totals
        token_row_block, codes_per_row, gradient_rows, up_weight_rows, table_row_list = block
        input_total = input_total.at[table_row_list].add(jnp.einsum("rk,rd->rkd", gradient_rows.astype(jnp.float32), token_row_block.astype(jnp.float32)))
        output_total = output_total.at[table_row_list].add(jnp.einsum("rk,rf->rkf", codes_per_row.astype(jnp.float32), up_weight_rows.astype(jnp.float32)))
        return (input_total, output_total), None

    start_totals = (jnp.zeros((ADAPTER_COUNT, ADAPTER_RANK, MODEL_WIDTH), jnp.float32), jnp.zeros((ADAPTER_COUNT, ADAPTER_RANK, HIDDEN_UNITS), jnp.float32))
    running_totals, unused = lax.scan(add_grads, start_totals, (token_blocks, code_blocks, gradient_blocks, up_weight_blocks, table_row_blocks))
    adapter_input_gradient = running_totals[0].astype(jnp.bfloat16)
    adapter_output_gradient = (adapter_scale * running_totals[1]).astype(jnp.bfloat16)
    return (layer_output, input_gradient, adapter_input_gradient, adapter_output_gradient)
```

```python
import functools

import jax
import jax.numpy as jnp
from jax import lax
from jax.experimental import pallas as pl
from jax.experimental.pallas import tpu as pltpu
from jax.sharding import PartitionSpec as P

adapter_scale = 0.5
lane = 128
f32 = jnp.float32
bf16 = jnp.bfloat16


def bit_count(n):
    bits = n.bit_length() - 1
    assert n == 1 << bits
    return bits


def bit_swap(x, axis, bit):
    n = lax.axis_size(axis)
    return lax.ppermute(x, axis, [(i, i ^ (1 << bit)) for i in range(n)])


def to_local(x, axis):
    n = lax.axis_size(axis)
    bits = bit_count(n)
    me = lax.axis_index(axis)
    tail = x.shape[1:]
    x = x.reshape((2,) * bits + tail)
    for dim in range(bits):
        odd = (me >> (bits - 1 - dim)) & 1
        x = jnp.where(odd == 0, x, jnp.flip(x, dim))
    x = jnp.transpose(x, tuple(range(bits))[::-1] + tuple(range(bits, x.ndim)))
    return x.reshape((n,) + tail)


def local_sum(x, axis):
    for bit in range(bit_count(lax.axis_size(axis))):
        half = x.shape[0] // 2
        x = x[:half] + bit_swap(x[half:], axis, bit)
    return x


def nn(x, y):
    return jnp.dot(x, y, preferred_element_type=f32)


def nt(x, y):
    return lax.dot_general(x, y, (((1,), (1,)), ((), ())), preferred_element_type=f32)


def both_of(*conds):
    conds = [cond for cond in conds if cond is not None]
    return functools.reduce(jnp.logical_and, conds) if conds else None


def run_if(cond, body):
    if cond is None:
        body()
    else:
        pl.when(cond)(body)


class Route:
    def __init__(self, lines, rows):
        self.kinds, self.lines, self.sizes = [], [], [rows]
        for line, length in lines:
            assert length in (2, 4)
            for kind in ["chain"] * (length // 2 - 1) + ["swap"]:
                self.kinds.append(kind)
                self.lines.append((line, length))
                self.sizes.append(self.sizes[-1] // 2 if kind == "swap" else self.sizes[-1])
        self.count = len(self.kinds)

    def arrive_rows(self):
        return self.sizes[1:]

    def send_rows(self):
        return self.sizes[1:]

    def place(self, me, minor):
        self.active, self.low = [None], [0]
        self.peer, self.near, self.far, self.keep = [], [], [], []
        for j in range(self.count):
            line, length = self.lines[j]
            pos = me % minor if line == 0 else me // minor
            step = 1 if line == 0 else minor
            upper = pos // (length // 2)
            active = self.active[-1]
            if self.kinds[j] == "chain":
                inner = jnp.logical_or(pos == length // 2 - 1, pos == length // 2)
                self.near.append(both_of(active, inner))
                self.far.append(both_of(active, jnp.logical_not(inner)))
                outward = 1 - 2 * (pos % 2)
                self.peer.append(me + outward * step)
                self.active.append(both_of(active, inner))
                self.low.append(self.low[-1])
                self.keep.append(None)
            else:
                self.near.append(active)
                self.far.append(active)
                self.peer.append(me + (1 - 2 * upper) * step)
                self.active.append(active)
                self.keep.append(upper)
                self.low.append(self.low[-1] + upper * self.sizes[j + 1])


def layer_kernel(axis, minor, parts, wide, chunks, keep_slots, ring, *refs):
    refs = list(refs)

    def take(count):
        taken, refs[:count] = refs[:count], []
        return taken

    tok, grad, code, gate_up, down, table = take(6)
    layer, inward, code_t, up_out = take(4)
    x2, own, full, acc_t = take(4)
    w_f, d_f, t_f, w_b, d_b, t_b = take(6)
    arrive = [take(route.count) for route, _, _ in parts]
    leave = [take(route.count) for route, _, _ in parts]
    sems = [take(4) for _ in parts]
    fwd_sem, bwd_sem, out_sem = take(3)
    rows, depth = tok.shape
    me = lax.axis_index(axis)
    peers = lax.axis_size(axis)
    for route, _, _ in parts:
        route.place(me, minor)

    barrier = pltpu.get_barrier_semaphore()
    for k in range(1, peers):
        pl.semaphore_signal(
            barrier, inc=1, device_id={axis: lax.rem(me + k, peers)},
            device_id_type=pl.DeviceIdType.MESH,
        )

    def columns(c):
        return pl.ds(pl.multiple_of(c * wide, wide), wide)

    def weight_copies(c, bufs, sem):
        slot = c % 2
        return [
            pltpu.make_async_copy(gate_up.at[:, :, columns(c)], bufs[0].at[slot], sem.at[slot, 0]),
            pltpu.make_async_copy(down.at[columns(c), :], bufs[1].at[slot], sem.at[slot, 1]),
            pltpu.make_async_copy(table.at[:, columns(c)], bufs[2].at[slot], sem.at[slot, 2]),
        ]

    def fetch_forward(c):
        for copy in weight_copies(c, (w_f, d_f, t_f), fwd_sem):
            copy.start()

    def fetch_backward(c):
        for copy in weight_copies(c, (w_b, d_b, t_b), bwd_sem):
            copy.start()

    def remote(src, dst, send_sem, recv_sem, peer):
        return pltpu.make_async_remote_copy(
            src_ref=src, dst_ref=dst, send_sem=send_sem, recv_sem=recv_sem,
            device_id={axis: peer}, device_id_type=pl.DeviceIdType.MESH,
        )

    def sum_copy(p, j, c):
        route = parts[p][0]
        sum_s, sum_r = sems[p][:2]
        return remote(
            leave[p][j].at[c % 2], arrive[p][j].at[c],
            sum_s.at[j, c % 2], sum_r.at[j, c % ring], route.peer[j],
        )

    def all_copy(p, m, c, mine):
        route, base, width = parts[p]
        j = route.count - 1 - m
        all_s, all_r = sems[p][2:]
        size = route.sizes[j + 1]
        if route.kinds[j] == "chain" or mine:
            low = route.low[j + 1]
        else:
            low = route.low[j] + (1 - route.keep[j]) * size
        at = full.at[c, :, pl.ds(align(low), size), pl.ds(base, width)]
        return remote(at, at, all_s.at[m, c % 2], all_r.at[m, c % ring], route.peer[j])

    def align(low):
        return low if isinstance(low, int) else pl.multiple_of(low, 16)

    def start_all(p, m, c):
        route = parts[p][0]
        pl.when(c >= 2)(lambda: all_copy(p, m, c - 2, True).wait_send())
        all_copy(p, m, c, True).start()
        j = route.count - 1 - m
        if route.kinds[j] == "chain" and m + 1 < route.count:
            start_all(p, m + 1, c)

    def sum_task(p, t, c):
        route, base, width = parts[p]
        cols = pl.ds(base, width)
        held = c % keep_slots

        def total(q, low, skip, size):
            value = own[held, q, pl.ds(align(low), size), cols]
            if t:
                value = value + arrive[p][t - 1][c, q, skip, :].astype(f32)
            return value

        def body():
            if t:
                sum_copy(p, t - 1, c).wait_recv()
            low, size = route.low[t], route.sizes[t]
            if t == route.count:
                every = pl.ds(0, size)
                gate_pre, up_pre, hidden_grad = [total(q, low, every, size) for q in range(3)]
                sig = jax.nn.sigmoid(gate_pre)
                act_gate = gate_pre * sig
                at = pl.ds(align(low), size)
                full[c, 2, at, cols] = (act_gate * up_pre).astype(bf16)
                full[c, 1, at, cols] = (hidden_grad * act_gate).astype(bf16)
                full[c, 0, at, cols] = (
                    hidden_grad * up_pre * sig * (1.0 + gate_pre * (1.0 - sig))
                ).astype(bf16)
                start_all(p, 0, c)
                return

            def ready():
                pl.when(c >= 2)(lambda: sum_copy(p, t, c - 2).wait_send())

            if route.kinds[t] == "chain":
                every = pl.ds(0, size)

                def send():
                    ready()
                    for q in range(3):
                        leave[p][t][c % 2, q] = total(q, low, every, size).astype(bf16)
                    sum_copy(p, t, c).start()

                run_if(route.far[t], send)
                if t:

                    def stay():
                        for q in range(3):
                            own[held, q, pl.ds(align(low), size), cols] = total(q, low, every, size)

                    run_if(route.near[t], stay)
            else:
                half, side = size // 2, route.keep[t]
                ready()
                skip = pl.ds(pl.multiple_of((1 - side) * half, 16), half)
                for q in range(3):
                    leave[p][t][c % 2, q] = total(q, low + (1 - side) * half, skip, half).astype(bf16)
                sum_copy(p, t, c).start()
                if t:
                    skip = pl.ds(pl.multiple_of(side * half, 16), half)
                    for q in range(3):
                        at = pl.ds(align(low + side * half), half)
                        own[held, q, at, cols] = total(q, low + side * half, skip, half)

        run_if(route.active[t], body)

    def all_task(p, m, c):
        route = parts[p][0]
        j = route.count - 1 - m

        def body():
            all_copy(p, m, c, False).wait_recv()
            if m + 1 < route.count:
                start_all(p, m + 1, c)

        if route.kinds[j] == "chain":
            run_if(route.far[j], body)
        else:
            run_if(route.active[j], body)

    def tasks(p, it):
        route = parts[p][0]
        for t in range(2 * route.count, -1, -1):
            c = it - t

            def go(t=t, c=c):
                if t <= route.count:
                    sum_task(p, t, c)
                else:
                    all_task(p, t - route.count - 1, c)

            pl.when(jnp.logical_and(c >= 0, c < chunks))(go)

    def forward(c):
        slot, held = c % 2, c % keep_slots
        for copy in weight_copies(c, (w_f, d_f, t_f), fwd_sem):
            copy.wait()
        pre = nn(x2[...], w_f.at[slot].reshape(2 * depth, wide)[...])
        own[held, 0] = pre[:rows]
        own[held, 1] = pre[rows:] + adapter_scale * nn(code[...], t_f[slot])
        own[held, 2] = nt(grad[...], d_f[slot])
        pl.when(c + 2 < chunks)(lambda: fetch_forward(c + 2))

    def out_copy(c):
        return pltpu.make_async_copy(
            full.at[c, 1], up_out.at[:, columns(c)], out_sem.at[c % 2]
        )

    def backward(c):
        slot = c % 2
        for copy in weight_copies(c, (w_b, d_b, t_b), bwd_sem):
            copy.wait()
        pl.when(c >= 2)(lambda: out_copy(c - 2).wait())
        out_copy(c).start()
        grads = full[c, 0:2].reshape(2 * rows, wide)
        weights = w_b.at[slot].reshape(2 * depth, wide)
        block = min(512, 2 * depth)

        def add(i, carry):
            at = pl.ds(pl.multiple_of(i * block, block), block)
            more = nt(weights[at, :], grads)
            for k in range(2 * rows // lane):
                acc_t[k, at, :] += more[:, lane * k : lane * (k + 1)]
            return carry

        lax.fori_loop(0, 2 * depth // block, add, 0)
        layer[...] += nn(full[c, 2], d_b[slot])
        code_t[...] += nt(t_b[slot], full[c, 1])
        pl.when(c + 2 < chunks)(lambda: fetch_backward(c + 2))

    for c in range(min(2, chunks)):
        fetch_forward(c)
        fetch_backward(c)
    row = lax.broadcasted_iota(jnp.int32, (lane, 2 * lane), 0)
    column = lax.broadcasted_iota(jnp.int32, (lane, 2 * lane), 1)
    for g in range(2):
        pick = (column == 2 * row + g).astype(f32).astype(bf16)
        for k in range(depth // lane):
            x2[g * rows : (g + 1) * rows, 2 * lane * k : 2 * lane * (k + 1)] = nn(
                tok[:, lane * k : lane * (k + 1)], pick
            ).astype(bf16)
    acc_t[...] = jnp.zeros_like(acc_t)
    layer[...] = jnp.zeros_like(layer)
    code_t[...] = jnp.zeros_like(code_t)
    forward(0)
    pl.semaphore_wait(barrier, peers - 1)
    lag = 2 * max(route.count for route, _, _ in parts)

    def step(it, carry):
        tasks(0, it)
        pl.when(it + 1 < chunks)(lambda: forward(it + 1))
        for p in range(1, len(parts)):
            tasks(p, it)
        pl.when(it >= lag)(lambda: backward(it - lag))
        return carry

    lax.fori_loop(0, chunks + lag, step, 0)
    half = rows // lane
    for k in range(half):
        inward[lane * k : lane * (k + 1), :] = (
            acc_t.at[k][pl.ds(0, depth, stride=2), :]
            + acc_t.at[half + k][pl.ds(1, depth, stride=2), :]
        ).T
    for c in range(max(chunks - 2, 0), chunks):
        out_copy(c).wait()
        for p, (route, _, _) in enumerate(parts):
            for j in range(route.count):
                run_if(route.far[j], lambda: sum_copy(p, j, c).wait_send())
                m = route.count - 1 - j
                run_if(route.near[j], lambda: all_copy(p, m, c, True).wait_send())


def layer_call(tok, grad, code, gate_up, down, table, axis):
    rows, depth = tok.shape
    hidden = down.shape[0]
    spread = table.shape[0]
    peers = lax.axis_size(axis)
    bits = bit_count(peers)
    minor = 1 << (bits // 2)
    major = peers // minor
    two = hidden % (2 * lane) == 0
    wide = 2 * lane if two else lane
    chunks = hidden // wide
    lines = [(0, minor), (1, major)]
    parts = [(Route(lines, rows), 0, lane)]
    if two:
        parts.append((Route(lines[::-1], rows), lane, lane))
    count = parts[0][0].count
    keep_slots, ring = count + 2, 2 * count + 2
    vmem = pl.BlockSpec(memory_space=pltpu.VMEM)
    anywhere = pl.BlockSpec(memory_space=pl.ANY)
    dma = pltpu.SemaphoreType.DMA
    scratch = [
        pltpu.VMEM((2 * rows, 2 * depth), bf16),
        pltpu.VMEM((keep_slots, 3, rows, wide), f32),
        pltpu.VMEM((chunks, 3, rows, wide), bf16),
        pltpu.VMEM((2 * rows // lane, 2 * depth, lane), f32),
    ]
    for _ in range(2):
        scratch += [
            pltpu.VMEM((2, depth, 2, wide), bf16),
            pltpu.VMEM((2, wide, depth), bf16),
            pltpu.VMEM((2, spread, wide), bf16),
        ]
    for route, _, width in parts:
        scratch += [pltpu.VMEM((chunks, 3, n, width), bf16) for n in route.arrive_rows()]
    for route, _, width in parts:
        scratch += [pltpu.VMEM((2, 3, n, width), bf16) for n in route.send_rows()]
    for _ in parts:
        scratch += [dma((count, 2)), dma((count, ring)), dma((count, 2)), dma((count, ring))]
    scratch += [dma((2, 3)), dma((2, 3)), dma((2,))]
    return pl.pallas_call(
        functools.partial(layer_kernel, axis, minor, parts, wide, chunks, keep_slots, ring),
        out_shape=[
            jax.ShapeDtypeStruct((rows, depth), f32),
            jax.ShapeDtypeStruct((rows, depth), f32),
            jax.ShapeDtypeStruct((spread, rows), f32),
            jax.ShapeDtypeStruct((rows, hidden), bf16),
        ],
        in_specs=[vmem] * 3 + [anywhere] * 3,
        out_specs=[vmem] * 3 + [anywhere],
        scratch_shapes=scratch,
        compiler_params=pltpu.CompilerParams(
            collective_id=0, has_side_effects=True, vmem_limit_bytes=67043328
        ),
    )(tok, grad, code, gate_up, down, table)


def sum_everywhere(x):
    for axis in ("tensor", "dp"):
        n = lax.axis_size(axis)
        if n & (n - 1):
            x = lax.psum(x, axis)
            continue
        bit = 1
        while bit < n:
            x = x + lax.ppermute(x, axis, [(i, i ^ bit) for i in range(n)])
            bit *= 2
    return x


def row_slots(request_token_rows, request_adapter, adapter_table_row, group_rows):
    request_count = request_token_rows.shape[1]
    run_ends = jnp.cumsum(request_token_rows, axis=1)
    position = jnp.arange(group_rows, dtype=jnp.int32)
    request_of = jnp.sum(
        (run_ends[:, None, :] <= position[None, :, None]).astype(jnp.int32), axis=2
    )
    adapter_ids = jnp.arange(adapter_table_row.shape[0], dtype=jnp.int32)
    table_row = jnp.sum(
        jnp.where(
            request_adapter[:, :, None] == adapter_ids[None, None, :],
            adapter_table_row[None, None, :],
            0,
        ),
        axis=2,
    )
    request_ids = jnp.arange(request_count, dtype=jnp.int32)
    return jnp.sum(
        jnp.where(request_of[:, :, None] == request_ids, table_row[:, None, :], 0), axis=2
    )


def slot_mask(slots, first_row, table_rows, rank):
    column = lax.broadcasted_iota(jnp.int32, (slots.shape[0], table_rows * rank), 1)
    return column // rank == (slots - first_row)[:, None]


def rank_spread(table_rows, rank, dtype):
    column = lax.broadcasted_iota(jnp.int32, (rank, table_rows * rank), 1)
    row = lax.broadcasted_iota(jnp.int32, (rank, table_rows * rank), 0)
    return (column % rank == row).astype(dtype)


def spread_codes(codes, mask, rank):
    spread = rank_spread(mask.shape[1] // rank, rank, bf16)
    tiled = jnp.dot(codes, spread, preferred_element_type=f32)
    return jnp.where(mask, tiled, 0.0).astype(bf16)


def fold_codes(full, mask, rank):
    spread = rank_spread(mask.shape[1] // rank, rank, f32)
    kept = jnp.where(mask, full, 0.0)
    return lax.dot_general(
        kept, spread, (((1,), (1,)), ((), ())), precision=lax.Precision.HIGHEST
    )


def on_device(
    tokens,
    output_gradient,
    gate_up_weight,
    down_weight,
    adapter_input_factor,
    adapter_output_factor,
    request_token_rows,
    request_adapter,
    adapter_table_row,
):
    group_rows = tokens.shape[0]
    groups = lax.axis_size("dp")
    rows = groups * group_rows
    rank = adapter_input_factor.shape[1]
    hidden_portion, width = down_weight.shape
    in_rows = adapter_input_factor.shape[0]
    out_rows = adapter_output_factor.shape[0]
    in_table = adapter_input_factor.reshape(in_rows * rank, width)
    out_table = adapter_output_factor.reshape(out_rows * rank, hidden_portion)

    def spread_rows(x):
        return lax.all_to_all(x, "dp", split_axis=1, concat_axis=0, tiled=True)

    token_cols = spread_rows(tokens)
    grad_cols = spread_rows(output_gradient)
    slots = row_slots(request_token_rows, request_adapter, adapter_table_row, group_rows)
    slots = slots.reshape(rows)
    in_mask = slot_mask(slots, lax.axis_index("tensor") * in_rows, in_rows, rank)
    out_mask = slot_mask(slots, lax.axis_index("dp") * out_rows, out_rows, rank)

    def total_codes(partial):
        return sum_everywhere(partial.reshape(groups, group_rows * rank)).reshape(rows, rank)

    all_codes = lax.dot_general(
        token_cols, in_table, (((1,), (1,)), ((), ())), preferred_element_type=f32
    )
    code_low = total_codes(fold_codes(all_codes, in_mask, rank)).astype(bf16)
    code_wide = spread_codes(code_low, out_mask, rank)

    layer_part, input_part, code_part_t, up_grad = layer_call(
        token_cols, grad_cols, code_wide, gate_up_weight, down_weight, out_table, "dp"
    )

    def finish(part):
        owners = lax.axis_size("tensor")
        part = to_local(part.reshape(owners, rows // owners, width), "tensor")
        return local_sum(part.reshape(rows, width), "tensor").astype(bf16)

    layer_output = finish(layer_part)
    code_grad = adapter_scale * total_codes(fold_codes(code_part_t.T, out_mask, rank))
    grad_wide = spread_codes(code_grad.astype(bf16), in_mask, rank)
    input_part = input_part + jnp.dot(grad_wide, in_table, preferred_element_type=f32)
    input_gradient = finish(input_part)
    adapter_input_gradient = lax.dot_general(
        grad_wide, token_cols, (((0,), (0,)), ((), ())), preferred_element_type=f32
    ).astype(bf16).reshape(in_rows, rank, width)
    adapter_output_gradient = (
        adapter_scale
        * lax.dot_general(
            code_wide, up_grad, (((0,), (0,)), ((), ())), preferred_element_type=f32
        )
    ).astype(bf16).reshape(out_rows, rank, hidden_portion)
    return (layer_output, input_gradient, adapter_input_gradient, adapter_output_gradient)


def solution(mesh):
    in_specs = (
        P("dp", None),
        P("dp", None),
        P("dp", None, "tensor"),
        P("tensor", "dp"),
        P("tensor", None, "dp"),
        P("dp", None, "tensor"),
        P(),
        P(),
        P(),
    )
    out_specs = (
        P("tensor", "dp"),
        P("tensor", "dp"),
        P("tensor", None, "dp"),
        P("dp", None, "tensor"),
    )
    return jax.shard_map(
        on_device, mesh=mesh, in_specs=in_specs, out_specs=out_specs, check_vma=False
    )
```

```python
import functools

import jax
import jax.numpy as jnp
from jax import lax
from jax.experimental import pallas as pl
from jax.experimental.pallas import tpu as pltpu
from jax.sharding import PartitionSpec as P

adapter_scale = 0.5
lane = 128
f32 = jnp.float32
bf16 = jnp.bfloat16


def bit_count(n):
    bits = n.bit_length() - 1
    assert n == 1 << bits
    return bits


def bit_swap(x, axis, bit):
    n = lax.axis_size(axis)
    return lax.ppermute(x, axis, [(i, i ^ (1 << bit)) for i in range(n)])


def to_local(x, axis):
    n = lax.axis_size(axis)
    bits = bit_count(n)
    me = lax.axis_index(axis)
    tail = x.shape[1:]
    x = x.reshape((2,) * bits + tail)
    for dim in range(bits):
        odd = (me >> (bits - 1 - dim)) & 1
        x = jnp.where(odd == 0, x, jnp.flip(x, dim))
    x = jnp.transpose(x, tuple(range(bits))[::-1] + tuple(range(bits, x.ndim)))
    return x.reshape((n,) + tail)


def local_sum(x, axis):
    for bit in range(bit_count(lax.axis_size(axis))):
        half = x.shape[0] // 2
        x = x[:half] + bit_swap(x[half:], axis, bit)
    return x


def nn(x, y):
    return jnp.dot(x, y, preferred_element_type=f32)


def nt(x, y):
    return lax.dot_general(x, y, (((1,), (1,)), ((), ())), preferred_element_type=f32)


def both_of(*conds):
    conds = [cond for cond in conds if cond is not None]
    return functools.reduce(jnp.logical_and, conds) if conds else None


def run_if(cond, body):
    if cond is None:
        body()
    else:
        pl.when(cond)(body)


class Route:
    def __init__(self, lines, rows):
        self.kinds, self.lines, self.sizes = [], [], [rows]
        for line, length in lines:
            assert length in (2, 4)
            for kind in ["chain"] * (length // 2 - 1) + ["swap"]:
                self.kinds.append(kind)
                self.lines.append((line, length))
                self.sizes.append(self.sizes[-1] // 2 if kind == "swap" else self.sizes[-1])
        self.count = len(self.kinds)

    def arrive_rows(self):
        return self.sizes[1:]

    def send_rows(self):
        return self.sizes[1:]

    def place(self, me, minor):
        self.active, self.low = [None], [0]
        self.peer, self.near, self.far, self.keep = [], [], [], []
        for j in range(self.count):
            line, length = self.lines[j]
            pos = me % minor if line == 0 else me // minor
            step = 1 if line == 0 else minor
            upper = pos // (length // 2)
            active = self.active[-1]
            if self.kinds[j] == "chain":
                inner = jnp.logical_or(pos == length // 2 - 1, pos == length // 2)
                self.near.append(both_of(active, inner))
                self.far.append(both_of(active, jnp.logical_not(inner)))
                outward = 1 - 2 * (pos % 2)
                self.peer.append(me + outward * step)
                self.active.append(both_of(active, inner))
                self.low.append(self.low[-1])
                self.keep.append(None)
            else:
                self.near.append(active)
                self.far.append(active)
                self.peer.append(me + (1 - 2 * upper) * step)
                self.active.append(active)
                self.keep.append(upper)
                self.low.append(self.low[-1] + upper * self.sizes[j + 1])


def layer_kernel(axes, share, minor, parts, wide, chunks, keep_slots, ring, *refs):
    refs = list(refs)

    def take(count):
        taken, refs[:count] = refs[:count], []
        return taken

    lengths, adapters, table_row, tok_rows, grad_rows, gate_up, down, in_table, table = take(9)
    tok, code_wide_t, grad_wide_t, layer, inward, up_out = take(6)
    grad, code, code_t, in_buf, slot_ref = take(5)
    x2, own, full, acc_t = take(4)
    w_f, d_f, t_f, w_b, d_b, t_b = take(6)
    arrive = [take(route.count) for route, _, _ in parts]
    leave = [take(route.count) for route, _, _ in parts]
    sems = [take(4) for _ in parts]
    fwd_sem, bwd_sem, out_sem = take(3)
    sum_tensor, sum_dp, code_part = take(3)
    in_sem, own_sem, row_s, row_r, share_s, share_r, ten_s, ten_r, dp_s, dp_r = take(10)
    axis, across = axes
    rows, depth = tok.shape
    group_rows = tok_rows.shape[0]
    in_count, rank = in_table.shape[:2]
    out_count = table.shape[0] // rank
    me = lax.axis_index(axis)
    peers = lax.axis_size(axis)
    side = lax.axis_index(across)
    sides = lax.axis_size(across)
    piece = depth // share
    for route, _, _ in parts:
        route.place(me, minor)

    barrier = pltpu.get_barrier_semaphore()
    for k in range(1, peers):
        pl.semaphore_signal(
            barrier, inc=1, device_id={axis: lax.rem(me + k, peers)},
            device_id_type=pl.DeviceIdType.MESH,
        )
    for k in range(1, sides):
        pl.semaphore_signal(
            barrier, inc=1, device_id={across: lax.rem(side + k, sides)},
            device_id_type=pl.DeviceIdType.MESH,
        )

    def columns(c):
        return pl.ds(pl.multiple_of(c * wide, wide), wide)

    def weight_copies(c, bufs, sem):
        slot = c % 2
        return [
            pltpu.make_async_copy(gate_up.at[:, :, columns(c)], bufs[0].at[slot], sem.at[slot, 0]),
            pltpu.make_async_copy(down.at[columns(c), :], bufs[1].at[slot], sem.at[slot, 1]),
            pltpu.make_async_copy(table.at[:, columns(c)], bufs[2].at[slot], sem.at[slot, 2]),
        ]

    def fetch_forward(c):
        for copy in weight_copies(c, (w_f, d_f, t_f), fwd_sem):
            copy.start()

    def fetch_backward(c):
        for copy in weight_copies(c, (w_b, d_b, t_b), bwd_sem):
            copy.start()

    def remote(src, dst, send_sem, recv_sem, peer, name=axis):
        return pltpu.make_async_remote_copy(
            src_ref=src, dst_ref=dst, send_sem=send_sem, recv_sem=recv_sem,
            device_id={name: peer}, device_id_type=pl.DeviceIdType.MESH,
        )

    sources, targets = (tok_rows, grad_rows), (tok, grad)

    def group_at(k):
        return pl.ds(pl.multiple_of(k * group_rows, group_rows), group_rows)

    def piece_at(k, base=0):
        return pl.ds(pl.multiple_of(base + k * piece, lane), piece)

    def row_copy(a, k, sent):
        peer = lax.rem(me + k, peers)
        owner = me if sent else peer
        part = side % share
        return remote(
            sources[a].at[:, piece_at(part, peer * depth)],
            targets[a].at[group_at(owner), piece_at(part)],
            row_s.at[a, k], row_r.at[a, owner], peer,
        )

    def own_copy(a):
        part = side % share
        return pltpu.make_async_copy(
            sources[a].at[:, piece_at(part, me * depth)],
            targets[a].at[group_at(me), piece_at(part)],
            own_sem.at[a],
        )

    def flip(k, bit):
        return k + bit * (1 - 2 * (k // bit % 2))

    share_steps, masks = [], [0]
    for level in range(bit_count(share) - 1, -1, -1):
        share_steps.append((1 << level, list(masks)))
        masks += [m ^ (1 << level) for m in masks]

    def share_copies(a, level, sent):
        bit, held = share_steps[level]
        copies = []
        for n, mask in enumerate(held):
            part = side % share
            for b in range(bit_count(share)):
                if (mask if sent else mask ^ bit) >> b & 1:
                    part = flip(part, 1 << b)
            at = targets[a].at[:, piece_at(part)]
            index = len(held) - 1 + n
            copies.append(
                remote(at, at, share_s.at[a, index], share_r.at[a, index], flip(side, bit), across)
            )
        return copies

    def code_copy(use, k, name, sent):
        if name == across:
            me_at, size, buf, send, recv = side, sides, sum_tensor, ten_s, ten_r
        else:
            me_at, size, buf, send, recv = me, peers, sum_dp, dp_s, dp_r
        peer = lax.rem(me_at + k, size)
        owner = me_at if sent else peer
        return remote(
            code_part.at[use, 0 if name == across else 1], buf.at[use, owner],
            send.at[use, k], recv.at[use, owner], peer, name,
        )

    def code_send(use, name, value):
        code_part[use, 0 if name == across else 1] = value
        for k in range(1, sides if name == across else peers):
            code_copy(use, k, name, True).start()

    def code_sum(use, name):
        size = sides if name == across else peers
        buf = sum_tensor if name == across else sum_dp
        me_at = side if name == across else me
        buf[use, me_at] = code_part[use, 0 if name == across else 1]
        for k in range(1, size):
            code_copy(use, k, name, False).wait_recv()
        value = buf[use, 0]
        for k in range(1, size):
            value = value + buf[use, k]
        return value

    def folded(block, count, read):
        def add(i, carry):
            ids = lax.broadcasted_iota(jnp.int32, (block, rank, rows), 0) + i * block
            kept = jnp.where(ids == slot_here[None], read(i), 0.0)
            return carry + jnp.sum(kept, axis=0)

        return lax.fori_loop(0, count // block, add, jnp.zeros((rank, rows), f32))

    def widen(block, count, value, write):
        def put(i, carry):
            ids = lax.broadcasted_iota(jnp.int32, (block, rank, rows), 0) + i * block
            kept = jnp.where(ids == slot_here[None], value[None], 0.0)
            write(i, kept.reshape(block * rank, rows).astype(bf16))
            return carry

        lax.fori_loop(0, count // block, put, 0)

    def sum_copy(p, j, c):
        route = parts[p][0]
        sum_s, sum_r = sems[p][:2]
        return remote(
            leave[p][j].at[c % 2], arrive[p][j].at[c],
            sum_s.at[j, c % 2], sum_r.at[j, c % ring], route.peer[j],
        )

    def all_copy(p, m, c, mine):
        route, base, width = parts[p]
        j = route.count - 1 - m
        all_s, all_r = sems[p][2:]
        size = route.sizes[j + 1]
        if route.kinds[j] == "chain" or mine:
            low = route.low[j + 1]
        else:
            low = route.low[j] + (1 - route.keep[j]) * size
        at = full.at[c, :, pl.ds(align(low), size), pl.ds(base, width)]
        return remote(at, at, all_s.at[m, c % 2], all_r.at[m, c % ring], route.peer[j])

    def align(low):
        return low if isinstance(low, int) else pl.multiple_of(low, 16)

    def start_all(p, m, c):
        route = parts[p][0]
        pl.when(c >= 2)(lambda: all_copy(p, m, c - 2, True).wait_send())
        all_copy(p, m, c, True).start()
        j = route.count - 1 - m
        if route.kinds[j] == "chain" and m + 1 < route.count:
            start_all(p, m + 1, c)

    def sum_task(p, t, c):
        route, base, width = parts[p]
        cols = pl.ds(base, width)
        held = c % keep_slots

        def total(q, low, skip, size):
            value = own[held, q, pl.ds(align(low), size), cols]
            if t:
                value = value + arrive[p][t - 1][c, q, skip, :].astype(f32)
            return value

        def body():
            if t:
                sum_copy(p, t - 1, c).wait_recv()
            low, size = route.low[t], route.sizes[t]
            if t == route.count:
                every = pl.ds(0, size)
                gate_pre, up_pre, hidden_grad = [total(q, low, every, size) for q in range(3)]
                sig = jax.nn.sigmoid(gate_pre)
                act_gate = gate_pre * sig
                at = pl.ds(align(low), size)
                full[c, 2, at, cols] = (act_gate * up_pre).astype(bf16)
                full[c, 1, at, cols] = (hidden_grad * act_gate).astype(bf16)
                full[c, 0, at, cols] = (
                    hidden_grad * up_pre * sig * (1.0 + gate_pre * (1.0 - sig))
                ).astype(bf16)
                start_all(p, 0, c)
                return

            def ready():
                pl.when(c >= 2)(lambda: sum_copy(p, t, c - 2).wait_send())

            if route.kinds[t] == "chain":
                every = pl.ds(0, size)

                def send():
                    ready()
                    for q in range(3):
                        leave[p][t][c % 2, q] = total(q, low, every, size).astype(bf16)
                    sum_copy(p, t, c).start()

                run_if(route.far[t], send)
                if t:

                    def stay():
                        for q in range(3):
                            own[held, q, pl.ds(align(low), size), cols] = total(q, low, every, size)

                    run_if(route.near[t], stay)
            else:
                half, side = size // 2, route.keep[t]
                ready()
                skip = pl.ds(pl.multiple_of((1 - side) * half, 16), half)
                for q in range(3):
                    leave[p][t][c % 2, q] = total(q, low + (1 - side) * half, skip, half).astype(bf16)
                sum_copy(p, t, c).start()
                if t:
                    skip = pl.ds(pl.multiple_of(side * half, 16), half)
                    for q in range(3):
                        at = pl.ds(align(low + side * half), half)
                        own[held, q, at, cols] = total(q, low + side * half, skip, half)

        run_if(route.active[t], body)

    def all_task(p, m, c):
        route = parts[p][0]
        j = route.count - 1 - m

        def body():
            all_copy(p, m, c, False).wait_recv()
            if m + 1 < route.count:
                start_all(p, m + 1, c)

        if route.kinds[j] == "chain":
            run_if(route.far[j], body)
        else:
            run_if(route.active[j], body)

    def tasks(p, it):
        route = parts[p][0]
        for t in range(2 * route.count, -1, -1):
            c = it - t

            def go(t=t, c=c):
                if t <= route.count:
                    sum_task(p, t, c)
                else:
                    all_task(p, t - route.count - 1, c)

            pl.when(jnp.logical_and(c >= 0, c < chunks))(go)

    def forward_inward(c):
        slot, held = c % 2, c % keep_slots
        gate_copy, _, table_copy = weight_copies(c, (w_f, d_f, t_f), fwd_sem)
        gate_copy.wait()
        pre = nn(x2[...], w_f.at[slot].reshape(2 * depth, wide)[...])
        own[held, 0] = pre[:rows]
        own[held, 1] = pre[rows:]

    def forward_hidden(c):
        slot, held = c % 2, c % keep_slots
        weight_copies(c, (w_f, d_f, t_f), fwd_sem)[1].wait()
        own[held, 2] = nt(grad[...], d_f[slot])

    def forward_lift(c):
        slot, held = c % 2, c % keep_slots
        weight_copies(c, (w_f, d_f, t_f), fwd_sem)[2].wait()
        own[held, 1] += adapter_scale * nn(code[...], t_f[slot])
        pl.when(c + 2 < chunks)(lambda: fetch_forward(c + 2))

    def forward(c):
        forward_inward(c)
        forward_hidden(c)
        forward_lift(c)

    def out_copy(c):
        return pltpu.make_async_copy(
            full.at[c, 1], up_out.at[:, columns(c)], out_sem.at[c % 2]
        )

    def backward(c):
        slot = c % 2
        for copy in weight_copies(c, (w_b, d_b, t_b), bwd_sem):
            copy.wait()
        pl.when(c >= 2)(lambda: out_copy(c - 2).wait())
        out_copy(c).start()
        grads = full[c, 0:2].reshape(2 * rows, wide)
        weights = w_b.at[slot].reshape(2 * depth, wide)
        block = min(512, 2 * depth)

        def add(i, carry):
            at = pl.ds(pl.multiple_of(i * block, block), block)
            more = nt(weights[at, :], grads)
            for k in range(2 * rows // lane):
                acc_t[k, at, :] += more[:, lane * k : lane * (k + 1)]
            return carry

        lax.fori_loop(0, 2 * depth // block, add, 0)
        layer[...] += nn(full[c, 2], d_b[slot])
        code_t[...] += nt(t_b[slot], full[c, 1])
        pl.when(c + 2 < chunks)(lambda: fetch_backward(c + 2))

    for c in range(min(2, chunks)):
        fetch_forward(c)
    in_copy = pltpu.make_async_copy(in_table, in_buf, in_sem)
    in_copy.start()
    for a in range(2):
        own_copy(a).start()
    pl.semaphore_wait(barrier, peers - 1 + sides - 1)
    for a in range(2):
        for k in range(1, peers):
            row_copy(a, k, True).start()
    spot = lax.broadcasted_iota(jnp.int32, (rank, rows), 1)
    slots = jnp.zeros((rank, rows), jnp.int32)
    for k in range(peers):
        first = jnp.int32(k * group_rows)
        for q in range(lengths.shape[1]):
            last = first + lengths[k, q]
            inside = jnp.logical_and(spot >= first, spot < last)
            slots = jnp.where(inside, table_row[adapters[k, q]], slots)
            first = last
    slot_ref[...] = slots
    acc_t[...] = jnp.zeros_like(acc_t)
    layer[...] = jnp.zeros_like(layer)
    code_t[...] = jnp.zeros_like(code_t)
    for level in range(-1, len(share_steps)):
        for a in range(2):
            if level < 0:
                own_copy(a).wait()
                for k in range(1, peers):
                    row_copy(a, k, False).wait_recv()
            elif level + 1 < len(share_steps) or a == 0:
                for copy in share_copies(a, level, False):
                    copy.wait_recv()
            if level + 1 < len(share_steps):
                for copy in share_copies(a, level + 1, True):
                    copy.start()
    in_copy.wait()
    slot_here = slot_ref[...] - side * in_count
    block = min(32, in_count)

    def in_codes(i):
        at = pl.ds(i * block, block)
        return nt(in_buf[at].reshape(block * rank, depth), tok[...]).reshape(block, rank, rows)

    code_send(0, across, folded(block, in_count, in_codes))
    row = lax.broadcasted_iota(jnp.int32, (lane, 2 * lane), 0)
    column = lax.broadcasted_iota(jnp.int32, (lane, 2 * lane), 1)
    for g in range(2):
        pick = (column == 2 * row + g).astype(f32).astype(bf16)
        for k in range(depth // lane):
            x2[g * rows : (g + 1) * rows, 2 * lane * k : 2 * lane * (k + 1)] = nn(
                tok[:, lane * k : lane * (k + 1)], pick
            ).astype(bf16)
    code_send(0, axis, code_sum(0, across))
    forward_inward(0)
    if share_steps:
        for copy in share_copies(1, len(share_steps) - 1, False):
            copy.wait_recv()
    forward_hidden(0)
    code_low = code_sum(0, axis).astype(bf16).astype(f32)
    slot_here = slot_ref[...] - me * out_count
    block = min(32, out_count)

    def put_code(i, value):
        code_wide_t[pl.ds(pl.multiple_of(i * block * rank, block * rank), block * rank), :] = value

    widen(block, out_count, code_low, put_code)
    code[...] = code_wide_t[...].T
    forward_lift(0)
    for c in range(min(2, chunks)):
        fetch_backward(c)
    lag = 2 * max(route.count for route, _, _ in parts)

    def step(it, carry):
        tasks(0, it)
        pl.when(it + 1 < chunks)(lambda: forward(it + 1))
        for p in range(1, len(parts)):
            tasks(p, it)
        pl.when(it >= lag)(lambda: backward(it - lag))
        return carry

    lax.fori_loop(0, chunks + lag, step, 0)
    slot_here = slot_ref[...] - me * out_count
    block = min(32, out_count)

    def out_codes(i):
        at = pl.ds(pl.multiple_of(i * block * rank, block * rank), block * rank)
        return code_t[at, :].reshape(block, rank, rows)

    code_send(1, across, folded(block, out_count, out_codes))
    half = rows // lane
    for k in range(half):
        inward[lane * k : lane * (k + 1), :] = (
            acc_t.at[k][pl.ds(0, depth, stride=2), :]
            + acc_t.at[half + k][pl.ds(1, depth, stride=2), :]
        ).T
        if k == 0:
            code_send(1, axis, code_sum(1, across))
    code_grad = (adapter_scale * code_sum(1, axis)).astype(bf16).astype(f32)
    slot_here = slot_ref[...] - side * in_count
    block = min(32, in_count)

    def put_grad(i, value):
        grad_wide_t[pl.ds(pl.multiple_of(i * block * rank, block * rank), block * rank), :] = value

    widen(block, in_count, code_grad, put_grad)
    for a in range(2):
        for k in range(1, peers):
            row_copy(a, k, True).wait_send()
        for level in range(len(share_steps)):
            for copy in share_copies(a, level, True):
                copy.wait_send()
    for use in range(2):
        for k in range(1, sides):
            code_copy(use, k, across, True).wait_send()
        for k in range(1, peers):
            code_copy(use, k, axis, True).wait_send()
    for c in range(max(chunks - 2, 0), chunks):
        out_copy(c).wait()
        for p, (route, _, _) in enumerate(parts):
            for j in range(route.count):
                run_if(route.far[j], lambda: sum_copy(p, j, c).wait_send())
                m = route.count - 1 - j
                run_if(route.near[j], lambda: all_copy(p, m, c, True).wait_send())


def layer_call(lengths, adapters, table_row, tokens, grads, gate_up, down, in_table, table, axes):
    hidden, depth = down.shape
    spread = table.shape[0]
    in_count, rank = in_table.shape[:2]
    peers, sides = [lax.axis_size(axis) for axis in axes]
    rows = peers * tokens.shape[0]
    share = min(sides, max(depth // lane, 1))
    bits = bit_count(peers)
    minor = 1 << (bits // 2)
    major = peers // minor
    two = hidden % (2 * lane) == 0
    wide = 2 * lane if two else lane
    chunks = hidden // wide
    lines = [(0, minor), (1, major)]
    parts = [(Route(lines, rows), 0, lane)]
    if two:
        parts.append((Route(lines[::-1], rows), lane, lane))
    count = parts[0][0].count
    keep_slots, ring = count + 2, 2 * count + 2
    vmem = pl.BlockSpec(memory_space=pltpu.VMEM)
    anywhere = pl.BlockSpec(memory_space=pl.ANY)
    dma = pltpu.SemaphoreType.DMA
    scratch = [
        pltpu.VMEM((rows, depth), bf16),
        pltpu.VMEM((rows, spread), bf16),
        pltpu.VMEM((spread, rows), f32),
        pltpu.VMEM(in_table.shape, bf16),
        pltpu.VMEM((rank, rows), jnp.int32),
        pltpu.VMEM((2 * rows, 2 * depth), bf16),
        pltpu.VMEM((keep_slots, 3, rows, wide), f32),
        pltpu.VMEM((chunks, 3, rows, wide), bf16),
        pltpu.VMEM((2 * rows // lane, 2 * depth, lane), f32),
    ]
    for _ in range(2):
        scratch += [
            pltpu.VMEM((2, depth, 2, wide), bf16),
            pltpu.VMEM((2, wide, depth), bf16),
            pltpu.VMEM((2, spread, wide), bf16),
        ]
    for route, _, width in parts:
        scratch += [pltpu.VMEM((chunks, 3, n, width), bf16) for n in route.arrive_rows()]
    for route, _, width in parts:
        scratch += [pltpu.VMEM((2, 3, n, width), bf16) for n in route.send_rows()]
    for _ in parts:
        scratch += [dma((count, 2)), dma((count, ring)), dma((count, 2)), dma((count, ring))]
    scratch += [dma((2, 3)), dma((2, 3)), dma((2,))]
    scratch += [
        pltpu.VMEM((2, sides, rank, rows), f32),
        pltpu.VMEM((2, peers, rank, rows), f32),
        pltpu.VMEM((2, 2, rank, rows), f32),
        dma, dma((2,)), dma((2, peers)), dma((2, peers)), dma((2, share)), dma((2, share)),
        dma((2, sides)), dma((2, sides)), dma((2, peers)), dma((2, peers)),
    ]
    smem = pl.BlockSpec(memory_space=pltpu.SMEM)
    return pl.pallas_call(
        functools.partial(layer_kernel, axes, share, minor, parts, wide, chunks, keep_slots, ring),
        out_shape=[
            jax.ShapeDtypeStruct((rows, depth), bf16),
            jax.ShapeDtypeStruct((spread, rows), bf16),
            jax.ShapeDtypeStruct((in_count * rank, rows), bf16),
            jax.ShapeDtypeStruct((rows, depth), f32),
            jax.ShapeDtypeStruct((rows, depth), f32),
            jax.ShapeDtypeStruct((rows, hidden), bf16),
        ],
        in_specs=[smem] * 3 + [anywhere] * 6,
        out_specs=[vmem] * 5 + [anywhere],
        scratch_shapes=scratch,
        compiler_params=pltpu.CompilerParams(
            collective_id=0, has_side_effects=True, vmem_limit_bytes=67043328
        ),
    )(lengths, adapters, table_row, tokens, grads, gate_up, down, in_table, table)


def on_device(
    tokens,
    output_gradient,
    gate_up_weight,
    down_weight,
    adapter_input_factor,
    adapter_output_factor,
    request_token_rows,
    request_adapter,
    adapter_table_row,
):
    rank = adapter_input_factor.shape[1]
    hidden_portion, width = down_weight.shape
    in_rows = adapter_input_factor.shape[0]
    out_rows = adapter_output_factor.shape[0]
    in_table = adapter_input_factor.reshape(in_rows * rank, width)
    out_table = adapter_output_factor.reshape(out_rows * rank, hidden_portion)
    token_cols, code_wide_t, grad_wide_t, layer_part, input_part, up_grad = layer_call(
        request_token_rows, request_adapter, adapter_table_row, tokens, output_gradient,
        gate_up_weight, down_weight, adapter_input_factor, out_table, ("dp", "tensor"),
    )
    rows = token_cols.shape[0]

    def finish(part):
        owners = lax.axis_size("tensor")
        part = to_local(part.reshape(owners, rows // owners, width), "tensor")
        return local_sum(part.reshape(rows, width), "tensor").astype(bf16)

    layer_output = finish(layer_part)
    input_part = input_part + lax.dot_general(
        grad_wide_t, in_table, (((0,), (0,)), ((), ())), preferred_element_type=f32
    )
    input_gradient = finish(input_part)
    adapter_input_gradient = nn(grad_wide_t, token_cols).astype(bf16)
    adapter_input_gradient = adapter_input_gradient.reshape(in_rows, rank, width)
    adapter_output_gradient = (adapter_scale * nn(code_wide_t, up_grad)).astype(bf16)
    adapter_output_gradient = adapter_output_gradient.reshape(out_rows, rank, hidden_portion)
    return (layer_output, input_gradient, adapter_input_gradient, adapter_output_gradient)


def solution(mesh):
    in_specs = (
        P("dp", None),
        P("dp", None),
        P("dp", None, "tensor"),
        P("tensor", "dp"),
        P("tensor", None, "dp"),
        P("dp", None, "tensor"),
        P(),
        P(),
        P(),
    )
    out_specs = (
        P("tensor", "dp"),
        P("tensor", "dp"),
        P("tensor", None, "dp"),
        P("dp", None, "tensor"),
    )
    return jax.shard_map(
        on_device, mesh=mesh, in_specs=in_specs, out_specs=out_specs, check_vma=False
    )
```

```python
import functools

import jax
import jax.numpy as jnp
from jax import lax
from jax.experimental import pallas as pl
from jax.experimental.pallas import tpu as pltpu
from jax.sharding import PartitionSpec as P

adapter_scale = 0.5
lane = 128
ends = (12, 12)
f32 = jnp.float32
bf16 = jnp.bfloat16


def bit_count(n):
    bits = n.bit_length() - 1
    assert n == 1 << bits
    return bits


def nn(x, y):
    return jnp.dot(x, y, preferred_element_type=f32)


def nt(x, y):
    return lax.dot_general(x, y, (((1,), (1,)), ((), ())), preferred_element_type=f32)


def both_of(*conds):
    conds = [cond for cond in conds if cond is not None]
    return functools.reduce(jnp.logical_and, conds) if conds else None


def run_if(cond, body):
    if cond is None:
        body()
    else:
        pl.when(cond)(body)


class Part:
    def __init__(self, route, base, width, first, last, chunks, inside):
        self.route, self.base, self.width = route, base, width
        self.first, self.last, self.inside = first, last, inside
        self.count = last - first if inside else chunks - (last - first)

    def holds(self, c):
        within = jnp.logical_and(c >= self.first, c < self.last)
        return within if self.inside else jnp.logical_not(within)

    def local(self, c):
        if self.inside:
            return c - self.first
        return jnp.where(c < self.first, c, c - (self.last - self.first))


class Route:
    def __init__(self, lines, rows):
        self.kinds, self.lines, self.sizes = [], [], [rows]
        for line, length in lines:
            assert length in (2, 4)
            for kind in ["chain"] * (length // 2 - 1) + ["swap"]:
                self.kinds.append(kind)
                self.lines.append((line, length))
                self.sizes.append(self.sizes[-1] // 2 if kind == "swap" else self.sizes[-1])
        self.count = len(self.kinds)

    def place(self, me, minor):
        self.active, self.low = [None], [0]
        self.peer, self.near, self.far, self.keep = [], [], [], []
        for j in range(self.count):
            line, length = self.lines[j]
            pos = me % minor if line == 0 else me // minor
            step = 1 if line == 0 else minor
            upper = pos // (length // 2)
            active = self.active[-1]
            if self.kinds[j] == "chain":
                inner = jnp.logical_or(pos == length // 2 - 1, pos == length // 2)
                self.near.append(both_of(active, inner))
                self.far.append(both_of(active, jnp.logical_not(inner)))
                outward = 1 - 2 * (pos % 2)
                self.peer.append(me + outward * step)
                self.active.append(both_of(active, inner))
                self.low.append(self.low[-1])
                self.keep.append(None)
            else:
                self.near.append(active)
                self.far.append(active)
                self.peer.append(me + (1 - 2 * upper) * step)
                self.active.append(active)
                self.keep.append(upper)
                self.low.append(self.low[-1] + upper * self.sizes[j + 1])


def layer_kernel(axes, share, minor, parts, wide, chunks, keep_slots, ring, *refs):
    refs = list(refs)

    def take(count):
        taken, refs[:count] = refs[:count], []
        return taken

    lengths, adapters, table_row, tok_rows, grad_rows, gate_up, down, in_table, table = take(9)
    tok, code_wide_t, grad_wide_t, layer_out, inward_out, up_out = take(6)
    layer, inward, grad, code, code_t, in_buf, slot_ref, which_ref = take(8)
    need_s, need_r, mine_ref, red32, red16_s, red16_r = take(6)
    x2, own, full, acc_t = take(4)
    w_f, d_f, t_f, w_b, d_b, t_b = take(6)
    routes = [part.route for part in parts]
    arrive = [take(route.count) for route in routes]
    leave = [take(route.count) for route in routes]
    sems = [take(4) for _ in parts]
    fwd_sem, bwd_sem, out_sem = take(3)
    sum_tensor, sum_dp, code_part = take(3)
    in_sem, own_sem, row_s, row_r, share_s, share_r, ten_s, ten_r, dp_s, dp_r = take(10)
    need_ss, need_rs, red_s, red_r = take(4)
    axis, across = axes
    rows, depth = tok.shape
    group_rows = tok_rows.shape[0]
    in_count, rank = in_table.shape[:2]
    out_count = table.shape[0] // rank
    me = lax.axis_index(axis)
    peers = lax.axis_size(axis)
    side = lax.axis_index(across)
    sides = lax.axis_size(across)
    piece = depth // share
    own_rows = rows // sides
    requests = lengths.shape[0]
    needed = peers // sides * requests
    for route in routes:
        route.place(me, minor)

    barrier = pltpu.get_barrier_semaphore()
    for k in range(1, peers):
        pl.semaphore_signal(
            barrier, inc=1, device_id={axis: lax.rem(me + k, peers)},
            device_id_type=pl.DeviceIdType.MESH,
        )
    for k in range(1, sides):
        pl.semaphore_signal(
            barrier, inc=1, device_id={across: lax.rem(side + k, sides)},
            device_id_type=pl.DeviceIdType.MESH,
        )

    def columns(c):
        return pl.ds(pl.multiple_of(c * wide, wide), wide)

    def weight_copies(c, bufs, sem):
        slot = c % 2
        return [
            pltpu.make_async_copy(gate_up.at[:, :, columns(c)], bufs[0].at[slot], sem.at[slot, 0]),
            pltpu.make_async_copy(down.at[columns(c), :], bufs[1].at[slot], sem.at[slot, 1]),
            pltpu.make_async_copy(table.at[:, columns(c)], bufs[2].at[slot], sem.at[slot, 2]),
        ]

    def fetch_forward(c):
        for copy in weight_copies(c, (w_f, d_f, t_f), fwd_sem):
            copy.start()

    def fetch_backward(c):
        for copy in weight_copies(c, (w_b, d_b, t_b), bwd_sem):
            copy.start()

    def remote(src, dst, send_sem, recv_sem, peer, name=axis):
        return pltpu.make_async_remote_copy(
            src_ref=src, dst_ref=dst, send_sem=send_sem, recv_sem=recv_sem,
            device_id={name: peer}, device_id_type=pl.DeviceIdType.MESH,
        )

    sources, targets = (tok_rows, grad_rows), (tok, grad)

    def group_at(k):
        return pl.ds(pl.multiple_of(k * group_rows, group_rows), group_rows)

    def piece_at(k, base=0):
        return pl.ds(pl.multiple_of(base + k * piece, lane), piece)

    def row_copy(a, k, sent):
        peer = lax.rem(me + k, peers)
        owner = me if sent else peer
        part = side % share
        return remote(
            sources[a].at[:, piece_at(part, peer * depth)],
            targets[a].at[group_at(owner), piece_at(part)],
            row_s.at[a, k], row_r.at[a, owner], peer,
        )

    def own_copy(a):
        part = side % share
        return pltpu.make_async_copy(
            sources[a].at[:, piece_at(part, me * depth)],
            targets[a].at[group_at(me), piece_at(part)],
            own_sem.at[a],
        )

    def flip(k, bit):
        return k + bit * (1 - 2 * (k // bit % 2))

    share_steps, masks = [], [0]
    for level in range(bit_count(share) - 1, -1, -1):
        share_steps.append((1 << level, list(masks)))
        masks += [m ^ (1 << level) for m in masks]

    def share_copies(a, level, sent):
        bit, held = share_steps[level]
        copies = []
        for n, mask in enumerate(held):
            part = side % share
            for b in range(bit_count(share)):
                if (mask if sent else mask ^ bit) >> b & 1:
                    part = flip(part, 1 << b)
            at = targets[a].at[:, piece_at(part)]
            index = len(held) - 1 + n
            copies.append(
                remote(at, at, share_s.at[a, index], share_r.at[a, index], flip(side, bit), across)
            )
        return copies

    def code_copy(use, k, name, sent):
        if name == across:
            me_at, size, buf, send, recv = side, sides, sum_tensor, ten_s, ten_r
        else:
            me_at, size, buf, send, recv = me, peers, sum_dp, dp_s, dp_r
        peer = lax.rem(me_at + k, size)
        owner = me_at if sent else peer
        return remote(
            code_part.at[use, 0 if name == across else 1], buf.at[use, owner],
            send.at[use, k], recv.at[use, owner], peer, name,
        )

    def code_send(use, name, value):
        code_part[use, 0 if name == across else 1] = value
        for k in range(1, sides if name == across else peers):
            code_copy(use, k, name, True).start()

    def code_sum(use, name):
        size = sides if name == across else peers
        buf = sum_tensor if name == across else sum_dp
        me_at = side if name == across else me
        buf[use, me_at] = code_part[use, 0 if name == across else 1]
        for k in range(1, size):
            code_copy(use, k, name, False).wait_recv()
        value = buf[use, 0]
        for k in range(1, size):
            value = value + buf[use, k]
        return value

    def need_copy(k, sent):
        peer = lax.rem(side + k, sides)
        owner = side if sent else peer
        return remote(
            need_s.at[peer], need_r.at[owner], need_ss.at[k], need_rs.at[owner], peer, across
        )

    def other(mask):
        place = side
        for b in range(bit_count(sides)):
            if mask >> b & 1:
                place = flip(place, 1 << b)
        return place

    sums = (layer, inward)

    def block_of(a, mask):
        at = pl.ds(pl.multiple_of(other(mask) * own_rows, own_rows), own_rows)
        return sums[a].at[at, :]

    def masks_of(b):
        return [m for m in range(1, sides) if m & -m == 1 << b]

    later = [m for m in range(1, sides) if m % 2 == 0]

    def reduce_copy(a, mask):
        if mask % 2:
            source, target = block_of(a, mask), red32.at[a, mask // 2]
        else:
            source, target = [buf.at[a, later.index(mask)] for buf in (red16_s, red16_r)]
        return remote(
            source, target, red_s.at[a, mask], red_r.at[a, mask], flip(side, mask & -mask), across
        )

    def reduce_start(a, b):
        for mask in masks_of(b):
            if b:
                red16_s[a, later.index(mask)] = block_of(a, mask)[...].astype(bf16)
            reduce_copy(a, mask).start()

    def reduce_end(a, b):
        for mask in masks_of(b):
            reduce_copy(a, mask).wait_recv()
            more = red32[a, mask // 2] if b == 0 else red16_r[a, later.index(mask)].astype(f32)
            block_of(a, mask ^ (1 << b))[...] += more

    def folded(block, count, read):
        def add(i, carry):
            ids = lax.broadcasted_iota(jnp.int32, (block, rank, rows), 0) + i * block
            kept = jnp.where(ids == slot_here[None], read(i), 0.0)
            return carry + jnp.sum(kept, axis=0)

        return lax.fori_loop(0, count // block, add, jnp.zeros((rank, rows), f32))

    def widen(block, count, value, write):
        def put(i, carry):
            ids = lax.broadcasted_iota(jnp.int32, (block, rank, rows), 0) + i * block
            kept = jnp.where(ids == slot_here[None], value[None], 0.0)
            write(i, kept.reshape(block * rank, rows).astype(bf16))
            return carry

        lax.fori_loop(0, count // block, put, 0)

    def sum_copy(p, j, n):
        sum_s, sum_r = sems[p][:2]
        return remote(
            leave[p][j].at[n % 2], arrive[p][j].at[n % ring],
            sum_s.at[j, n % 2], sum_r.at[j, n % ring], routes[p].peer[j],
        )

    def all_copy(p, m, c, n, mine):
        route, base, width = routes[p], parts[p].base, parts[p].width
        j = route.count - 1 - m
        all_s, all_r = sems[p][2:]
        size = route.sizes[j + 1]
        if route.kinds[j] == "chain" or mine:
            low = route.low[j + 1]
        else:
            low = route.low[j] + (1 - route.keep[j]) * size
        at = full.at[c, :, pl.ds(align(low), size), pl.ds(base, width)]
        return remote(at, at, all_s.at[m, n % 2], all_r.at[m, n % ring], route.peer[j])

    def align(low):
        return low if isinstance(low, int) else pl.multiple_of(low, 16)

    def start_all(p, m, c):
        route, n = routes[p], parts[p].local(c)
        pl.when(n >= 2)(lambda: all_copy(p, m, c, n, True).wait_send())
        all_copy(p, m, c, n, True).start()
        j = route.count - 1 - m
        if route.kinds[j] == "chain" and m + 1 < route.count:
            start_all(p, m + 1, c)

    def sum_task(p, t, c):
        route, n = routes[p], parts[p].local(c)
        cols = pl.ds(parts[p].base, parts[p].width)
        held = c % keep_slots

        def total(q, low, skip, size):
            value = own[held, q, pl.ds(align(low), size), cols]
            if t:
                value = value + arrive[p][t - 1][n % ring, q, skip, :].astype(f32)
            return value

        def body():
            if t:
                sum_copy(p, t - 1, n).wait_recv()
            low, size = route.low[t], route.sizes[t]
            if t == route.count:
                every = pl.ds(0, size)
                gate_pre, up_pre, hidden_grad = [total(q, low, every, size) for q in range(3)]
                sig = jax.nn.sigmoid(gate_pre)
                act_gate = gate_pre * sig
                at = pl.ds(align(low), size)
                full[c, 2, at, cols] = (act_gate * up_pre).astype(bf16)
                full[c, 1, at, cols] = (hidden_grad * act_gate).astype(bf16)
                full[c, 0, at, cols] = (
                    hidden_grad * up_pre * sig * (1.0 + gate_pre * (1.0 - sig))
                ).astype(bf16)
                start_all(p, 0, c)
                return

            def ready():
                pl.when(n >= 2)(lambda: sum_copy(p, t, n).wait_send())

            if route.kinds[t] == "chain":
                every = pl.ds(0, size)

                def send():
                    ready()
                    for q in range(3):
                        leave[p][t][n % 2, q] = total(q, low, every, size).astype(bf16)
                    sum_copy(p, t, n).start()

                run_if(route.far[t], send)
                if t:

                    def stay():
                        for q in range(3):
                            own[held, q, pl.ds(align(low), size), cols] = total(q, low, every, size)

                    run_if(route.near[t], stay)
            else:
                half, side = size // 2, route.keep[t]
                ready()
                skip = pl.ds(pl.multiple_of((1 - side) * half, 16), half)
                for q in range(3):
                    leave[p][t][n % 2, q] = total(q, low + (1 - side) * half, skip, half).astype(bf16)
                sum_copy(p, t, n).start()
                if t:
                    skip = pl.ds(pl.multiple_of(side * half, 16), half)
                    for q in range(3):
                        at = pl.ds(align(low + side * half), half)
                        own[held, q, at, cols] = total(q, low + side * half, skip, half)

        run_if(route.active[t], body)

    def all_task(p, m, c):
        route = routes[p]
        j = route.count - 1 - m

        def body():
            all_copy(p, m, c, parts[p].local(c), False).wait_recv()
            if m + 1 < route.count:
                start_all(p, m + 1, c)

        if route.kinds[j] == "chain":
            run_if(route.far[j], body)
        else:
            run_if(route.active[j], body)

    def tasks(p, it):
        route = routes[p]
        for t in range(2 * route.count, -1, -1):
            c = it - t

            def go(t=t, c=c):
                if t <= route.count:
                    sum_task(p, t, c)
                else:
                    all_task(p, t - route.count - 1, c)

            pl.when(both_of(c >= 0, c < chunks, parts[p].holds(c)))(go)

    def forward_inward(c):
        slot, held = c % 2, c % keep_slots
        gate_copy, _, table_copy = weight_copies(c, (w_f, d_f, t_f), fwd_sem)
        gate_copy.wait()
        pre = nn(x2[...], w_f.at[slot].reshape(2 * depth, wide)[...])
        own[held, 0] = pre[:rows]
        own[held, 1] = pre[rows:]

    def forward_hidden(c):
        slot, held = c % 2, c % keep_slots
        weight_copies(c, (w_f, d_f, t_f), fwd_sem)[1].wait()
        own[held, 2] = nt(grad[...], d_f[slot])

    def forward_lift(c):
        slot, held = c % 2, c % keep_slots
        weight_copies(c, (w_f, d_f, t_f), fwd_sem)[2].wait()
        own[held, 1] += adapter_scale * nn(code[...], t_f[slot])
        pl.when(c + 2 < chunks)(lambda: fetch_forward(c + 2))

    def forward(c):
        forward_inward(c)
        forward_hidden(c)
        forward_lift(c)

    def out_copy(c):
        return pltpu.make_async_copy(
            full.at[c, 1], up_out.at[:, columns(c)], out_sem.at[c % 2]
        )

    def backward(c):
        slot = c % 2
        for copy in weight_copies(c, (w_b, d_b, t_b), bwd_sem):
            copy.wait()
        pl.when(c >= 2)(lambda: out_copy(c - 2).wait())
        out_copy(c).start()
        grads = full[c, 0:2].reshape(2 * rows, wide)
        weights = w_b.at[slot].reshape(2 * depth, wide)
        block = min(512, 2 * depth)

        def add(i, carry):
            at = pl.ds(pl.multiple_of(i * block, block), block)
            more = nt(weights[at, :], grads)
            for k in range(2 * rows // lane):
                acc_t[k, at, :] += more[:, lane * k : lane * (k + 1)]
            return carry

        lax.fori_loop(0, 2 * depth // block, add, 0)
        layer[...] += nn(full[c, 2], d_b[slot])
        code_t[...] += nt(t_b[slot], full[c, 1])
        pl.when(c + 2 < chunks)(lambda: fetch_backward(c + 2))

    for c in range(min(2, chunks)):
        fetch_forward(c)
    in_copy = pltpu.make_async_copy(in_table, in_buf, in_sem)
    in_copy.start()
    for a in range(2):
        own_copy(a).start()
    pl.semaphore_wait(barrier, peers - 1 + sides - 1)
    for a in range(2):
        for k in range(1, peers):
            row_copy(a, k, True).start()
    spot = lax.broadcasted_iota(jnp.int32, (rank, rows), 1)
    slots = jnp.zeros((rank, rows), jnp.int32)
    which = jnp.zeros((rank, rows), jnp.int32)
    for k in range(peers):
        first = jnp.int32(k * group_rows)
        for q in range(lengths.shape[0]):
            last = first + lengths[q, k]
            inside = jnp.logical_and(spot >= first, spot < last)
            slots = jnp.where(inside, table_row[adapters[q, k]], slots)
            which = jnp.where(inside, k * requests + q, which)
            first = last
    slot_ref[...] = slots
    which_ref[...] = which
    acc_t[...] = jnp.zeros_like(acc_t)
    layer[...] = jnp.zeros_like(layer)
    code_t[...] = jnp.zeros_like(code_t)
    for level in range(-1, len(share_steps)):
        for a in range(2):
            if level < 0:
                own_copy(a).wait()
                for k in range(1, peers):
                    row_copy(a, k, False).wait_recv()
            elif level + 1 < len(share_steps) or a == 0:
                for copy in share_copies(a, level, False):
                    copy.wait_recv()
            if level + 1 < len(share_steps):
                for copy in share_copies(a, level + 1, True):
                    copy.start()
    in_copy.wait()
    slot_here = slot_ref[...] - side * in_count
    block = min(32, in_count)

    def in_codes(i):
        at = pl.ds(i * block, block)
        return nt(in_buf[at].reshape(block * rank, depth), tok[...]).reshape(block, rank, rows)

    code_send(0, across, folded(block, in_count, in_codes))
    row = lax.broadcasted_iota(jnp.int32, (lane, 2 * lane), 0)
    column = lax.broadcasted_iota(jnp.int32, (lane, 2 * lane), 1)
    for g in range(2):
        pick = (column == 2 * row + g).astype(f32).astype(bf16)
        for k in range(depth // lane):
            x2[g * rows : (g + 1) * rows, 2 * lane * k : 2 * lane * (k + 1)] = nn(
                tok[:, lane * k : lane * (k + 1)], pick
            ).astype(bf16)
    code_send(0, axis, code_sum(0, across))
    forward_inward(0)
    if share_steps:
        for copy in share_copies(1, len(share_steps) - 1, False):
            copy.wait_recv()
    forward_hidden(0)
    for s in range(sides):
        for i in range(needed):
            at = table_row[adapters[i % requests, s * (needed // requests) + i // requests]]
            at = at - side * in_count
            here = jnp.logical_and(at >= 0, at < in_count)
            row = in_buf[jnp.clip(at, 0, in_count - 1)].astype(f32)
            need_s[s, i] = jnp.where(here, row, 0.0).astype(bf16)
    for k in range(1, sides):
        need_copy(k, True).start()
    code_low = code_sum(0, axis).astype(bf16).astype(f32)
    slot_here = slot_ref[...] - me * out_count
    block = min(32, out_count)

    def put_code(i, value):
        code_wide_t[pl.ds(pl.multiple_of(i * block * rank, block * rank), block * rank), :] = value

    widen(block, out_count, code_low, put_code)
    code[...] = code_wide_t[...].T
    forward_lift(0)
    for c in range(min(2, chunks)):
        fetch_backward(c)
    lag = 2 * max(route.count for route in routes)

    def step(it, carry):
        tasks(0, it)
        pl.when(it + 1 < chunks)(lambda: forward(it + 1))
        for p in range(1, len(parts)):
            tasks(p, it)
        pl.when(it >= lag)(lambda: backward(it - lag))
        return carry

    lax.fori_loop(0, chunks + lag, step, 0)
    slot_here = slot_ref[...] - me * out_count
    block = min(32, out_count)

    def out_codes(i):
        at = pl.ds(pl.multiple_of(i * block * rank, block * rank), block * rank)
        return code_t[at, :].reshape(block, rank, rows)

    code_send(1, across, folded(block, out_count, out_codes))
    bits = bit_count(sides)
    if bits:
        reduce_start(0, 0)
    half = rows // lane
    for k in range(half):
        inward[lane * k : lane * (k + 1), :] = (
            acc_t.at[k][pl.ds(0, depth, stride=2), :]
            + acc_t.at[half + k][pl.ds(1, depth, stride=2), :]
        ).T
    if bits:
        reduce_start(1, 0)
    code_send(1, axis, code_sum(1, across))
    for b in range(bits):
        for a in range(2):
            reduce_end(a, b)
            if b + 1 < bits:
                reduce_start(a, b + 1)
            elif a == 0:
                layer_out[...] = block_of(0, 0)[...].astype(bf16)
    need = need_s[side].astype(f32)
    for k in range(1, sides):
        need_copy(k, False).wait_recv()
        need = need + need_r[lax.rem(side + k, sides)].astype(f32)
    need = need.reshape(needed * rank, depth).astype(bf16)
    code_grad = (adapter_scale * code_sum(1, axis)).astype(bf16).astype(f32)
    ids = lax.broadcasted_iota(jnp.int32, (needed, rank, rows), 0) + side * needed
    mine = jnp.where(ids == which_ref[...][None], code_grad[None], 0.0)
    mine_ref[...] = mine.reshape(needed * rank, rows).T
    own_at = pl.ds(pl.multiple_of(side * own_rows, own_rows), own_rows)
    term = nn(mine_ref[own_at, :].astype(bf16), need)
    inward_out[...] = (block_of(1, 0)[...] + term).astype(bf16)
    slot_here = slot_ref[...] - side * in_count
    block = min(32, in_count)

    def put_grad(i, value):
        grad_wide_t[pl.ds(pl.multiple_of(i * block * rank, block * rank), block * rank), :] = value

    widen(block, in_count, code_grad, put_grad)
    for k in range(1, sides):
        need_copy(k, True).wait_send()
    for a in range(2):
        for mask in range(1, sides):
            reduce_copy(a, mask).wait_send()
    for a in range(2):
        for k in range(1, peers):
            row_copy(a, k, True).wait_send()
        for level in range(len(share_steps)):
            for copy in share_copies(a, level, True):
                copy.wait_send()
    for use in range(2):
        for k in range(1, sides):
            code_copy(use, k, across, True).wait_send()
        for k in range(1, peers):
            code_copy(use, k, axis, True).wait_send()
    for c in range(max(chunks - 2, 0), chunks):
        out_copy(c).wait()
    for p, route in enumerate(routes):
        for n in range(max(parts[p].count - 2, 0), parts[p].count):
            for j in range(route.count):
                run_if(route.far[j], lambda: sum_copy(p, j, n).wait_send())
                m = route.count - 1 - j
                run_if(route.near[j], lambda: all_copy(p, m, 0, n, True).wait_send())


def layer_call(lengths, adapters, table_row, tokens, grads, gate_up, down, in_table, table, axes):
    hidden, depth = down.shape
    spread = table.shape[0]
    in_count, rank = in_table.shape[:2]
    peers, sides = [lax.axis_size(axis) for axis in axes]
    rows = peers * tokens.shape[0]
    share = min(sides, max(depth // lane, 1))
    bits = bit_count(peers)
    minor = 1 << (bits // 2)
    major = peers // minor
    two = hidden % (2 * lane) == 0
    wide = 2 * lane if two else lane
    chunks = hidden // wide
    lines = [(0, minor), (1, major)]
    parts = [Part(Route(lines, rows), 0, lane, 0, chunks, chunks, True)]
    if two:
        first, last = chunks * ends[0] // 100, chunks - chunks * ends[1] // 100
        parts.append(Part(Route(lines[::-1], rows), lane, lane, first, last, chunks, True))
        if parts[-1].count < chunks:
            parts.append(Part(Route(lines, rows), lane, lane, first, last, chunks, False))
    count = parts[0].route.count
    keep_slots, ring = count + 2, 2 * count + 2
    vmem = pl.BlockSpec(memory_space=pltpu.VMEM)
    anywhere = pl.BlockSpec(memory_space=pl.ANY)
    dma = pltpu.SemaphoreType.DMA
    own_rows = rows // sides
    needed = peers // sides * lengths.shape[0]
    later = max(sides // 2 - 1, 1)
    scratch = [
        pltpu.VMEM((rows, depth), f32),
        pltpu.VMEM((rows, depth), f32),
        pltpu.VMEM((rows, depth), bf16),
        pltpu.VMEM((rows, spread), bf16),
        pltpu.VMEM((spread, rows), f32),
        pltpu.VMEM(in_table.shape, bf16),
        pltpu.VMEM((rank, rows), jnp.int32),
        pltpu.VMEM((rank, rows), jnp.int32),
        pltpu.VMEM((sides, needed, rank, depth), bf16),
        pltpu.VMEM((sides, needed, rank, depth), bf16),
        pltpu.VMEM((rows, needed * rank), f32),
        pltpu.VMEM((2, max(sides // 2, 1), own_rows, depth), f32),
        pltpu.VMEM((2, later, own_rows, depth), bf16),
        pltpu.VMEM((2, later, own_rows, depth), bf16),
        pltpu.VMEM((2 * rows, 2 * depth), bf16),
        pltpu.VMEM((keep_slots, 3, rows, wide), f32),
        pltpu.VMEM((chunks, 3, rows, wide), bf16),
        pltpu.VMEM((2 * rows // lane, 2 * depth, lane), f32),
    ]
    for _ in range(2):
        scratch += [
            pltpu.VMEM((2, depth, 2, wide), bf16),
            pltpu.VMEM((2, wide, depth), bf16),
            pltpu.VMEM((2, spread, wide), bf16),
        ]
    for slots in (ring, 2):
        for part in parts:
            scratch += [pltpu.VMEM((slots, 3, n, part.width), bf16) for n in part.route.sizes[1:]]
    for _ in parts:
        scratch += [dma((count, 2)), dma((count, ring)), dma((count, 2)), dma((count, ring))]
    scratch += [dma((2, 3)), dma((2, 3)), dma((2,))]
    scratch += [
        pltpu.VMEM((2, sides, rank, rows), f32),
        pltpu.VMEM((2, peers, rank, rows), f32),
        pltpu.VMEM((2, 2, rank, rows), f32),
        dma, dma((2,)), dma((2, peers)), dma((2, peers)), dma((2, share)), dma((2, share)),
        dma((2, sides)), dma((2, sides)), dma((2, peers)), dma((2, peers)),
        dma((sides,)), dma((sides,)), dma((2, sides)), dma((2, sides)),
    ]
    smem = pl.BlockSpec(memory_space=pltpu.SMEM)
    return pl.pallas_call(
        functools.partial(layer_kernel, axes, share, minor, parts, wide, chunks, keep_slots, ring),
        out_shape=[
            jax.ShapeDtypeStruct((rows, depth), bf16),
            jax.ShapeDtypeStruct((spread, rows), bf16),
            jax.ShapeDtypeStruct((in_count * rank, rows), bf16),
            jax.ShapeDtypeStruct((own_rows, depth), bf16),
            jax.ShapeDtypeStruct((own_rows, depth), bf16),
            jax.ShapeDtypeStruct((rows, hidden), bf16),
        ],
        in_specs=[smem] * 3 + [anywhere] * 6,
        out_specs=[vmem] * 5 + [anywhere],
        scratch_shapes=scratch,
        compiler_params=pltpu.CompilerParams(
            collective_id=0, has_side_effects=True, vmem_limit_bytes=67043328
        ),
    )(lengths, adapters, table_row, tokens, grads, gate_up, down, in_table, table)


def on_device(
    tokens,
    output_gradient,
    gate_up_weight,
    down_weight,
    adapter_input_factor,
    adapter_output_factor,
    request_token_rows,
    request_adapter,
    adapter_table_row,
):
    rank = adapter_input_factor.shape[1]
    hidden_portion, width = down_weight.shape
    in_rows = adapter_input_factor.shape[0]
    out_rows = adapter_output_factor.shape[0]
    out_table = adapter_output_factor.reshape(out_rows * rank, hidden_portion)
    token_cols, code_wide_t, grad_wide_t, layer_output, input_gradient, up_grad = layer_call(
        request_token_rows.T, request_adapter.T, adapter_table_row, tokens, output_gradient,
        gate_up_weight, down_weight, adapter_input_factor, out_table, ("dp", "tensor"),
    )
    adapter_input_gradient = nn(grad_wide_t, token_cols).astype(bf16)
    adapter_input_gradient = adapter_input_gradient.reshape(in_rows, rank, width)
    adapter_output_gradient = (adapter_scale * nn(code_wide_t, up_grad)).astype(bf16)
    adapter_output_gradient = adapter_output_gradient.reshape(out_rows, rank, hidden_portion)
    return (layer_output, input_gradient, adapter_input_gradient, adapter_output_gradient)


def solution(mesh):
    in_specs = (
        P("dp", None),
        P("dp", None),
        P("dp", None, "tensor"),
        P("tensor", "dp"),
        P("tensor", None, "dp"),
        P("dp", None, "tensor"),
        P(),
        P(),
        P(),
    )
    out_specs = (
        P("tensor", "dp"),
        P("tensor", "dp"),
        P("tensor", None, "dp"),
        P("dp", None, "tensor"),
    )
    return jax.shard_map(
        on_device, mesh=mesh, in_specs=in_specs, out_specs=out_specs, check_vma=False
    )
```

```python
import functools

import jax
import jax.numpy as jnp
from jax import lax
from jax.experimental import pallas as pl
from jax.experimental.pallas import tpu as pltpu
from jax.sharding import PartitionSpec as P

adapter_scale = 0.5
lane = 128
pieces = 4
ends = (16, 16)
f32 = jnp.float32
bf16 = jnp.bfloat16


def bit_count(n):
    bits = n.bit_length() - 1
    assert n == 1 << bits
    return bits


def nn(x, y):
    return jnp.dot(x, y, preferred_element_type=f32)


def nt(x, y):
    return lax.dot_general(x, y, (((1,), (1,)), ((), ())), preferred_element_type=f32)


def both_of(*conds):
    conds = [cond for cond in conds if cond is not None]
    return functools.reduce(jnp.logical_and, conds) if conds else None


def run_if(cond, body):
    if cond is None:
        body()
    else:
        pl.when(cond)(body)


class Part:
    def __init__(self, route, base, width, first, last, chunks, inside):
        self.route, self.base, self.width = route, base, width
        self.first, self.last, self.inside = first, last, inside
        self.count = last - first if inside else chunks - (last - first)

    def holds(self, c):
        within = jnp.logical_and(c >= self.first, c < self.last)
        return within if self.inside else jnp.logical_not(within)

    def local(self, c):
        if self.inside:
            return c - self.first
        return jnp.where(c < self.first, c, c - (self.last - self.first))


class Route:
    def __init__(self, lines, rows):
        self.kinds, self.lines, self.sizes, self.sent, self.gives = [], [], [rows], [], []
        for line, length, give in lines:
            assert length in (2, 4)
            give = give and length == 4
            size = self.sizes[-1]
            kinds = ["chain"] * (length // 2 - 1) + ["swap"] + ["give"] * give
            after = {"chain": size, "swap": size // 2, "give": size // 4}
            for kind in kinds:
                self.kinds.append(kind)
                self.lines.append((line, length))
                self.gives.append(give)
                self.sizes.append(after[kind])
                self.sent.append(size - size // 4 if kind == "chain" and give else after[kind])
        self.count = len(self.kinds)

    def place(self, me, minor):
        self.active, self.low = [None], [0]
        self.peer, self.near, self.far, self.keep, self.cover = [], [], [], [], []
        for j in range(self.count):
            line, length = self.lines[j]
            pos = me % minor if line == 0 else me // minor
            step = 1 if line == 0 else minor
            upper = pos // (length // 2)
            active, low = self.active[-1], self.low[-1]
            inner = jnp.logical_or(pos == length // 2 - 1, pos == length // 2)
            outer = jnp.logical_not(inner)
            partner = me + (1 - 2 * (pos % 2)) * step
            self.keep.append(upper)
            self.cover.append(0)
            if self.kinds[j] == "chain":
                every, start = active, low
                self.near.append(both_of(active, inner))
                self.far.append(both_of(active, outer))
                self.peer.append(partner)
                self.active.append(both_of(active, inner))
                self.low.append(low)
                if self.gives[j]:
                    self.cover[-1] = low + (1 - upper) * (self.sizes[j] // 4)
                else:
                    self.cover[-1] = low
            elif self.kinds[j] == "swap":
                self.near.append(active)
                self.far.append(active)
                self.peer.append(me + (1 - 2 * upper) * step)
                self.active.append(active)
                self.low.append(low + upper * self.sizes[j + 1])
            else:
                self.near.append(both_of(every, outer))
                self.far.append(both_of(every, inner))
                self.peer.append(partner)
                self.active.append(every)
                self.low.append(start + pos * self.sizes[j + 1])
                self.cover[-1] = start + upper * 3 * self.sizes[j + 1]


def layer_kernel(axes, share, minor, parts, wide, chunks, keep_slots, ring, *refs):
    refs = list(refs)

    def take(count):
        taken, refs[:count] = refs[:count], []
        return taken

    lengths, adapters, table_row, tok_rows, grad_rows, gate_up, down, in_table, table = take(9)
    tok_out, code_out, grad_wide_t, layer_out, inward_out, up_out = take(6)
    tok, code_wide_t = take(2)
    layer, inward, grad, code, code_t, in_buf, slot_ref, which_ref = take(8)
    need_s, need_r, mine_ref, red32, red16_s, red16_r = take(6)
    x2, own, full, acc_t = take(4)
    w_f, d_f, t_f, w_b, d_b, t_b = take(6)
    routes = [part.route for part in parts]
    arrive = [take(route.count) for route in routes]
    leave = [take(route.count) for route in routes]
    sems = [take(4) for _ in parts]
    fwd_sem, bwd_sem, out_sem = take(3)
    sum_tensor, sum_dp, code_part = take(3)
    in_sem, own_sem, row_s, row_r, share_s, share_r, ten_s, ten_r, dp_s, dp_r = take(10)
    need_ss, need_rs, red_s, red_r, early_sem = take(5)
    axis, across = axes
    rows, depth = tok.shape
    group_rows = tok_rows.shape[0]
    in_count, rank = in_table.shape[:2]
    out_count = table.shape[0] // rank
    me = lax.axis_index(axis)
    peers = lax.axis_size(axis)
    side = lax.axis_index(across)
    sides = lax.axis_size(across)
    piece = depth // share
    own_rows = rows // sides
    requests = lengths.shape[0]
    needed = peers // sides * requests
    for route in routes:
        route.place(me, minor)

    barrier = pltpu.get_barrier_semaphore()
    for k in range(1, peers):
        pl.semaphore_signal(
            barrier, inc=1, device_id={axis: lax.rem(me + k, peers)},
            device_id_type=pl.DeviceIdType.MESH,
        )
    for k in range(1, sides):
        pl.semaphore_signal(
            barrier, inc=1, device_id={across: lax.rem(side + k, sides)},
            device_id_type=pl.DeviceIdType.MESH,
        )

    def columns(c):
        return pl.ds(pl.multiple_of(c * wide, wide), wide)

    def weight_copies(c, bufs, sem):
        slot = c % 2
        return [
            pltpu.make_async_copy(gate_up.at[:, :, columns(c)], bufs[0].at[slot], sem.at[slot, 0]),
            pltpu.make_async_copy(down.at[columns(c), :], bufs[1].at[slot], sem.at[slot, 1]),
            pltpu.make_async_copy(table.at[:, columns(c)], bufs[2].at[slot], sem.at[slot, 2]),
        ]

    def fetch_forward(c):
        for copy in weight_copies(c, (w_f, d_f, t_f), fwd_sem):
            copy.start()

    def fetch_backward(c):
        for copy in weight_copies(c, (w_b, d_b, t_b), bwd_sem):
            copy.start()

    def remote(src, dst, send_sem, recv_sem, peer, name=axis):
        return pltpu.make_async_remote_copy(
            src_ref=src, dst_ref=dst, send_sem=send_sem, recv_sem=recv_sem,
            device_id={name: peer}, device_id_type=pl.DeviceIdType.MESH,
        )

    sources, targets = (tok_rows, grad_rows), (tok, grad)

    def group_at(k):
        return pl.ds(pl.multiple_of(k * group_rows, group_rows), group_rows)

    def piece_at(k, base=0):
        return pl.ds(pl.multiple_of(base + k * piece, lane), piece)

    def row_copy(a, k, sent):
        peer = lax.rem(me + k, peers)
        owner = me if sent else peer
        part = side % share
        return remote(
            sources[a].at[:, piece_at(part, peer * depth)],
            targets[a].at[group_at(owner), piece_at(part)],
            row_s.at[a, k], row_r.at[a, owner], peer,
        )

    def own_copy(a):
        part = side % share
        return pltpu.make_async_copy(
            sources[a].at[:, piece_at(part, me * depth)],
            targets[a].at[group_at(me), piece_at(part)],
            own_sem.at[a],
        )

    def flip(k, bit):
        return k + bit * (1 - 2 * (k // bit % 2))

    share_steps, masks = [], [0]
    for level in range(bit_count(share) - 1, -1, -1):
        share_steps.append((1 << level, list(masks)))
        masks += [m ^ (1 << level) for m in masks]

    def share_copies(a, level, sent):
        bit, held = share_steps[level]
        copies = []
        for n, mask in enumerate(held):
            part = side % share
            for b in range(bit_count(share)):
                if (mask if sent else mask ^ bit) >> b & 1:
                    part = flip(part, 1 << b)
            at = targets[a].at[:, piece_at(part)]
            index = len(held) - 1 + n
            copies.append(
                remote(at, at, share_s.at[a, index], share_r.at[a, index], flip(side, bit), across)
            )
        return copies

    def code_copy(use, k, name, sent):
        if name == across:
            me_at, size, buf, send, recv = side, sides, sum_tensor, ten_s, ten_r
        else:
            me_at, size, buf, send, recv = me, peers, sum_dp, dp_s, dp_r
        peer = lax.rem(me_at + k, size)
        owner = me_at if sent else peer
        return remote(
            code_part.at[use, 0 if name == across else 1], buf.at[use, owner],
            send.at[use, k], recv.at[use, owner], peer, name,
        )

    def code_send(use, name, value):
        code_part[use, 0 if name == across else 1] = value
        for k in range(1, sides if name == across else peers):
            code_copy(use, k, name, True).start()

    def code_sum(use, name):
        size = sides if name == across else peers
        buf = sum_tensor if name == across else sum_dp
        me_at = side if name == across else me
        buf[use, me_at] = code_part[use, 0 if name == across else 1]
        for k in range(1, size):
            code_copy(use, k, name, False).wait_recv()
        value = buf[use, 0]
        for k in range(1, size):
            value = value + buf[use, k]
        return value

    def need_copy(k, sent):
        peer = lax.rem(side + k, sides)
        owner = side if sent else peer
        return remote(
            need_s.at[peer], need_r.at[owner], need_ss.at[k], need_rs.at[owner], peer, across
        )

    def other(mask):
        place = side
        for b in range(bit_count(sides)):
            if mask >> b & 1:
                place = flip(place, 1 << b)
        return place

    sums = (layer, inward)

    def block_of(a, mask):
        at = pl.ds(pl.multiple_of(other(mask) * own_rows, own_rows), own_rows)
        return sums[a].at[at, :]

    def masks_of(b):
        return [m for m in range(1, sides) if m & -m == 1 << b]

    later = [m for m in range(1, sides) if m % 2 == 0]

    def reduce_copy(a, mask):
        if mask % 2:
            source, target = block_of(a, mask), red32.at[a, mask // 2]
        else:
            source, target = [buf.at[a, later.index(mask)] for buf in (red16_s, red16_r)]
        return remote(
            source, target, red_s.at[a, mask], red_r.at[a, mask], flip(side, mask & -mask), across
        )

    def reduce_start(a, b):
        for mask in masks_of(b):
            if b:
                red16_s[a, later.index(mask)] = block_of(a, mask)[...].astype(bf16)
            reduce_copy(a, mask).start()

    def reduce_end(a, b):
        for mask in masks_of(b):
            reduce_copy(a, mask).wait_recv()
            more = red32[a, mask // 2] if b == 0 else red16_r[a, later.index(mask)].astype(f32)
            block_of(a, mask ^ (1 << b))[...] += more

    def folded(block, count, read):
        def add(i, carry):
            ids = lax.broadcasted_iota(jnp.int32, (block, rank, rows), 0) + i * block
            kept = jnp.where(ids == slot_here[None], read(i), 0.0)
            return carry + jnp.sum(kept, axis=0)

        return lax.fori_loop(0, count // block, add, jnp.zeros((rank, rows), f32))

    def widen(block, count, value, write):
        def put(i, carry):
            ids = lax.broadcasted_iota(jnp.int32, (block, rank, rows), 0) + i * block
            kept = jnp.where(ids == slot_here[None], value[None], 0.0)
            write(i, kept.reshape(block * rank, rows).astype(bf16))
            return carry

        lax.fori_loop(0, count // block, put, 0)

    def sum_copy(p, j, n):
        sum_s, sum_r = sems[p][:2]
        return remote(
            leave[p][j].at[n % 2], arrive[p][j].at[n % ring],
            sum_s.at[j, n % 2], sum_r.at[j, n % ring], routes[p].peer[j],
        )

    def all_copy(p, m, c, n, mine):
        route, base, width = routes[p], parts[p].base, parts[p].width
        j = route.count - 1 - m
        all_s, all_r = sems[p][2:]
        size = route.sent[j]
        if route.kinds[j] == "chain":
            low = route.cover[j]
        elif mine:
            low = route.low[j + 1]
        elif route.kinds[j] == "give":
            low = route.cover[j]
        else:
            low = route.low[j] + (1 - route.keep[j]) * size
        at = full.at[c, :, pl.ds(align(low), size), pl.ds(base, width)]
        return remote(at, at, all_s.at[m, n % 2], all_r.at[m, n % ring], route.peer[j])

    def align(low):
        return low if isinstance(low, int) else pl.multiple_of(low, 16)

    def start_all(p, m, c):
        route, n = routes[p], parts[p].local(c)
        j = route.count - 1 - m

        def body():
            pl.when(n >= 2)(lambda: all_copy(p, m, c, n, True).wait_send())
            all_copy(p, m, c, n, True).start()

        run_if(route.near[j] if route.kinds[j] == "give" else None, body)
        if route.kinds[j] == "chain" and m + 1 < route.count:
            start_all(p, m + 1, c)

    def sum_task(p, t, c):
        route, n = routes[p], parts[p].local(c)
        cols = pl.ds(parts[p].base, parts[p].width)
        held = c % keep_slots

        fresh = t > 0 and route.kinds[t - 1] != "give"

        def total(q, low, skip, size):
            value = own[held, q, pl.ds(align(low), size), cols]
            if fresh:
                at = pl.ds(skip if isinstance(skip, int) else pl.multiple_of(skip, 16), size)
                value = value + arrive[p][t - 1][n % ring, q, at, :].astype(f32)
            return value

        def ready():
            pl.when(n >= 2)(lambda: sum_copy(p, t, n).wait_send())

        def send(low, skip, size):
            ready()
            for q in range(3):
                leave[p][t][n % 2, q] = total(q, low, skip, size).astype(bf16)
            sum_copy(p, t, n).start()

        def stay(low, skip, size):
            if fresh:
                for q in range(3):
                    own[held, q, pl.ds(align(low), size), cols] = total(q, low, skip, size)

        def receive():
            sum_copy(p, t - 1, n).wait_recv()

        def body():
            low, size = route.low[t], route.sizes[t]
            if fresh:
                receive()
            elif t:

                def back():
                    receive()
                    for q in range(3):
                        own[held, q, pl.ds(align(low), size), cols] += arrive[p][t - 1][
                            n % ring, q
                        ].astype(f32)

                run_if(route.near[t - 1], back)
            if t == route.count:
                gate_pre, up_pre, hidden_grad = [total(q, low, 0, size) for q in range(3)]
                sig = jax.nn.sigmoid(gate_pre)
                act_gate = gate_pre * sig
                at = pl.ds(align(low), size)
                full[c, 2, at, cols] = (act_gate * up_pre).astype(bf16)
                full[c, 1, at, cols] = (hidden_grad * act_gate).astype(bf16)
                full[c, 0, at, cols] = (
                    hidden_grad * up_pre * sig * (1.0 + gate_pre * (1.0 - sig))
                ).astype(bf16)
                start_all(p, 0, c)
                return
            side = route.keep[t]
            if route.kinds[t] == "chain":
                skip = route.cover[t] - low
                run_if(route.far[t], lambda: send(route.cover[t], skip, route.sent[t]))
                if fresh:
                    run_if(route.near[t], lambda: stay(low, 0, size))
                return
            half = size // 2
            if route.kinds[t] == "give":
                send(low + side * half, side * half, half)
                stay(low + (1 - side) * half, (1 - side) * half, half)
            elif t and route.kinds[t - 1] == "chain" and route.gives[t - 1]:
                quarter = half // 2
                send(low + (1 - side) * half, (1 - side) * quarter, half)
                stay(low + quarter + side * quarter, side * half, quarter)
            else:
                send(low + (1 - side) * half, (1 - side) * half, half)
                stay(low + side * half, side * half, half)

        run_if(route.active[t], body)

    def all_task(p, m, c):
        route = routes[p]
        j = route.count - 1 - m

        def body():
            all_copy(p, m, c, parts[p].local(c), False).wait_recv()
            if m + 1 < route.count:
                start_all(p, m + 1, c)

        run_if(route.active[j] if route.kinds[j] == "swap" else route.far[j], body)

    def tasks(p, it):
        route = routes[p]
        for t in range(2 * route.count, -1, -1):
            c = it - t

            def go(t=t, c=c):
                if t <= route.count:
                    sum_task(p, t, c)
                else:
                    all_task(p, t - route.count - 1, c)

            pl.when(both_of(c >= 0, c < chunks, parts[p].holds(c)))(go)

    def forward_inward(c):
        slot, held = c % 2, c % keep_slots
        gate_copy, _, table_copy = weight_copies(c, (w_f, d_f, t_f), fwd_sem)
        gate_copy.wait()
        pre = nn(x2[...], w_f.at[slot].reshape(2 * depth, wide)[...])
        own[held, 0] = pre[:rows]
        own[held, 1] = pre[rows:]

    def forward_hidden(c):
        slot, held = c % 2, c % keep_slots
        weight_copies(c, (w_f, d_f, t_f), fwd_sem)[1].wait()
        own[held, 2] = nt(grad[...], d_f[slot])

    def forward_lift(c):
        slot, held = c % 2, c % keep_slots
        weight_copies(c, (w_f, d_f, t_f), fwd_sem)[2].wait()
        own[held, 1] += adapter_scale * nn(code[...], t_f[slot])
        pl.when(c + 2 < chunks)(lambda: fetch_forward(c + 2))

    def forward(c):
        forward_inward(c)
        forward_hidden(c)
        forward_lift(c)

    def out_copy(c):
        return pltpu.make_async_copy(
            full.at[c, 1], up_out.at[:, columns(c)], out_sem.at[c % 2]
        )

    def backward_layer(c):
        slot = c % 2
        weight_copies(c, (w_b, d_b, t_b), bwd_sem)[1].wait()
        layer[...] += nn(full[c, 2], d_b[slot])

    def backward_code(c):
        weight_copies(c, (w_b, d_b, t_b), bwd_sem)[2].wait()
        code_t[...] += nt(t_b[c % 2], full[c, 1])

    def backward_inward(c):
        slot = c % 2
        pl.when(c >= 2)(lambda: out_copy(c - 2).wait())
        out_copy(c).start()
        weight_copies(c, (w_b, d_b, t_b), bwd_sem)[0].wait()
        grads = full[c, 0:2].reshape(2 * rows, wide)
        weights = w_b.at[slot].reshape(2 * depth, wide)
        block = min(512, 2 * depth)

        def add(i, carry):
            at = pl.ds(pl.multiple_of(i * block, block), block)
            more = nt(weights[at, :], grads)
            for k in range(2 * rows // lane):
                acc_t[k, at, :] += more[:, lane * k : lane * (k + 1)]
            return carry

        lax.fori_loop(0, 2 * depth // block, add, 0)
        pl.when(c + 2 < chunks)(lambda: fetch_backward(c + 2))

    def backward(c):
        backward_code(c)
        backward_layer(c)
        backward_inward(c)

    for c in range(min(2, chunks)):
        fetch_forward(c)
    in_copy = pltpu.make_async_copy(in_table, in_buf, in_sem)
    in_copy.start()
    for a in range(2):
        own_copy(a).start()
    pl.semaphore_wait(barrier, peers - 1 + sides - 1)
    for a in range(2):
        for k in range(1, peers):
            row_copy(a, k, True).start()
    spot = lax.broadcasted_iota(jnp.int32, (rank, rows), 1)
    slots = jnp.zeros((rank, rows), jnp.int32)
    which = jnp.zeros((rank, rows), jnp.int32)
    for k in range(peers):
        first = jnp.int32(k * group_rows)
        for q in range(lengths.shape[0]):
            last = first + lengths[q, k]
            inside = jnp.logical_and(spot >= first, spot < last)
            slots = jnp.where(inside, table_row[adapters[q, k]], slots)
            which = jnp.where(inside, k * requests + q, which)
            first = last
    slot_ref[...] = slots
    which_ref[...] = which
    acc_t[...] = jnp.zeros_like(acc_t)
    layer[...] = jnp.zeros_like(layer)
    code_t[...] = jnp.zeros_like(code_t)
    in_copy.wait()
    for s in range(sides):
        for i in range(needed):
            at = table_row[adapters[i % requests, s * (needed // requests) + i // requests]]
            at = at - side * in_count
            here = jnp.logical_and(at >= 0, at < in_count)
            row = in_buf[jnp.clip(at, 0, in_count - 1)].astype(f32)
            need_s[s, i] = jnp.where(here, row, 0.0).astype(bf16)
    for level in range(-1, len(share_steps)):
        for a in range(2):
            if level < 0:
                own_copy(a).wait()
                for k in range(1, peers):
                    row_copy(a, k, False).wait_recv()
            elif level + 1 < len(share_steps) or a == 0:
                for copy in share_copies(a, level, False):
                    copy.wait_recv()
            if level + 1 < len(share_steps):
                for copy in share_copies(a, level + 1, True):
                    copy.start()
    every = sides * needed
    some = nt(need_s[...].reshape(every * rank, depth), tok[...]).reshape(every, rank, rows)
    ids = lax.broadcasted_iota(jnp.int32, (every, rank, rows), 0)
    code_send(0, across, jnp.sum(jnp.where(ids == which_ref[...][None], some, 0.0), axis=0))
    for k in range(1, sides):
        need_copy(k, True).start()
    row = lax.broadcasted_iota(jnp.int32, (lane, 2 * lane), 0)
    column = lax.broadcasted_iota(jnp.int32, (lane, 2 * lane), 1)
    for g in range(2):
        pick = (column == 2 * row + g).astype(f32).astype(bf16)
        for k in range(depth // lane):
            x2[g * rows : (g + 1) * rows, 2 * lane * k : 2 * lane * (k + 1)] = nn(
                tok[:, lane * k : lane * (k + 1)], pick
            ).astype(bf16)
    code_send(0, axis, code_sum(0, across))
    forward_inward(0)
    if share_steps:
        for copy in share_copies(1, len(share_steps) - 1, False):
            copy.wait_recv()
    forward_hidden(0)
    code_low = code_sum(0, axis).astype(bf16).astype(f32)
    slot_here = slot_ref[...] - me * out_count
    block = min(32, out_count)

    def put_code(i, value):
        code_wide_t[pl.ds(pl.multiple_of(i * block * rank, block * rank), block * rank), :] = value

    widen(block, out_count, code_low, put_code)
    code[...] = code_wide_t[...].T
    early = [
        pltpu.make_async_copy(tok, tok_out, early_sem.at[0]),
        pltpu.make_async_copy(code_wide_t, code_out, early_sem.at[1]),
    ]
    for copy in early:
        copy.start()
    forward_lift(0)
    for c in range(min(2, chunks)):
        fetch_backward(c)
    lag = 2 * max(route.count for route in routes)

    def step(it, carry):
        tasks(0, it)
        pl.when(it + 1 < chunks)(lambda: forward(it + 1))
        for p in range(1, len(parts)):
            tasks(p, it)
        pl.when(it >= lag)(lambda: backward(it - lag))
        return carry

    lax.fori_loop(0, chunks + lag - 1, step, 0)
    for p in range(len(parts)):
        tasks(p, jnp.int32(chunks + lag - 1))
    bits = bit_count(sides)
    backward_code(chunks - 1)
    slot_here = slot_ref[...] - me * out_count
    block = min(32, out_count)

    def out_codes(i):
        at = pl.ds(pl.multiple_of(i * block * rank, block * rank), block * rank)
        return code_t[at, :].reshape(block, rank, rows)

    code_send(1, across, folded(block, out_count, out_codes))
    backward_layer(chunks - 1)
    if bits:
        reduce_start(0, 0)
    backward_inward(chunks - 1)
    code_send(1, axis, code_sum(1, across))
    half = rows // lane
    for k in range(half):
        inward[lane * k : lane * (k + 1), :] = (
            acc_t.at[k][pl.ds(0, depth, stride=2), :]
            + acc_t.at[half + k][pl.ds(1, depth, stride=2), :]
        ).T
    if bits:
        reduce_start(1, 0)
    for b in range(bits - 1):
        for a in range(2):
            reduce_end(a, b)
            reduce_start(a, b + 1)
    for copy in early:
        copy.wait()
    need = need_s[side].astype(f32)
    for k in range(1, sides):
        need_copy(k, False).wait_recv()
        need = need + need_r[lax.rem(side + k, sides)].astype(f32)
    need = need.reshape(needed * rank, depth).astype(bf16)
    code_grad = (adapter_scale * code_sum(1, axis)).astype(bf16).astype(f32)
    ids = lax.broadcasted_iota(jnp.int32, (needed, rank, rows), 0) + side * needed
    mine = jnp.where(ids == which_ref[...][None], code_grad[None], 0.0)
    mine_ref[...] = mine.reshape(needed * rank, rows).T
    own_at = pl.ds(pl.multiple_of(side * own_rows, own_rows), own_rows)
    term = nn(mine_ref[own_at, :].astype(bf16), need)
    slot_here = slot_ref[...] - side * in_count
    block = min(32, in_count)

    def put_grad(i, value):
        grad_wide_t[pl.ds(pl.multiple_of(i * block * rank, block * rank), block * rank), :] = value

    widen(block, in_count, code_grad, put_grad)
    if bits:
        reduce_end(0, bits - 1)
    layer_out[...] = block_of(0, 0)[...].astype(bf16)
    if bits:
        reduce_end(1, bits - 1)
    inward_out[...] = (block_of(1, 0)[...] + term).astype(bf16)
    for k in range(1, sides):
        need_copy(k, True).wait_send()
    for a in range(2):
        for mask in range(1, sides):
            reduce_copy(a, mask).wait_send()
    for a in range(2):
        for k in range(1, peers):
            row_copy(a, k, True).wait_send()
        for level in range(len(share_steps)):
            for copy in share_copies(a, level, True):
                copy.wait_send()
    for use in range(2):
        for k in range(1, sides):
            code_copy(use, k, across, True).wait_send()
        for k in range(1, peers):
            code_copy(use, k, axis, True).wait_send()
    for c in range(max(chunks - 2, 0), chunks):
        out_copy(c).wait()
    for p, route in enumerate(routes):
        for n in range(max(parts[p].count - 2, 0), parts[p].count):
            for j in range(route.count):
                run_if(route.far[j], lambda: sum_copy(p, j, n).wait_send())
                m = route.count - 1 - j
                run_if(route.near[j], lambda: all_copy(p, m, 0, n, True).wait_send())


def layer_call(lengths, adapters, table_row, tokens, grads, gate_up, down, in_table, table, axes):
    hidden, depth = down.shape
    spread = table.shape[0]
    in_count, rank = in_table.shape[:2]
    peers, sides = [lax.axis_size(axis) for axis in axes]
    rows = peers * tokens.shape[0]
    share = min(sides, max(depth // lane, 1))
    bits = bit_count(peers)
    minor = 1 << (bits // 2)
    major = peers // minor
    two = hidden % (2 * lane) == 0
    wide = 2 * lane if two else lane
    chunks = hidden // wide
    lines = [(0, minor, False), (1, major, False)]
    turned = [(1, major, False), (0, minor, False)]
    parts = [Part(Route(lines, rows), 0, lane, 0, chunks, chunks, True)]
    if two:
        first, last = chunks * ends[0] // 100, chunks - chunks * ends[1] // 100
        parts.append(Part(Route(turned, rows), lane, lane, first, last, chunks, True))
        if parts[-1].count < chunks:
            parts.append(Part(Route(lines, rows), lane, lane, first, last, chunks, False))
    count = max(part.route.count for part in parts)
    keep_slots, ring = count + 2, 2 * count + 2
    vmem = pl.BlockSpec(memory_space=pltpu.VMEM)
    anywhere = pl.BlockSpec(memory_space=pl.ANY)
    dma = pltpu.SemaphoreType.DMA
    own_rows = rows // sides
    needed = peers // sides * lengths.shape[0]
    later = max(sides // 2 - 1, 1)
    scratch = [
        pltpu.VMEM((rows, depth), bf16),
        pltpu.VMEM((spread, rows), bf16),
        pltpu.VMEM((rows, depth), f32),
        pltpu.VMEM((rows, depth), f32),
        pltpu.VMEM((rows, depth), bf16),
        pltpu.VMEM((rows, spread), bf16),
        pltpu.VMEM((spread, rows), f32),
        pltpu.VMEM(in_table.shape, bf16),
        pltpu.VMEM((rank, rows), jnp.int32),
        pltpu.VMEM((rank, rows), jnp.int32),
        pltpu.VMEM((sides, needed, rank, depth), bf16),
        pltpu.VMEM((sides, needed, rank, depth), bf16),
        pltpu.VMEM((rows, needed * rank), f32),
        pltpu.VMEM((2, max(sides // 2, 1), own_rows, depth), f32),
        pltpu.VMEM((2, later, own_rows, depth), bf16),
        pltpu.VMEM((2, later, own_rows, depth), bf16),
        pltpu.VMEM((2 * rows, 2 * depth), bf16),
        pltpu.VMEM((keep_slots, 3, rows, wide), f32),
        pltpu.VMEM((chunks, 3, rows, wide), bf16),
        pltpu.VMEM((2 * rows // lane, 2 * depth, lane), f32),
    ]
    for _ in range(2):
        scratch += [
            pltpu.VMEM((2, depth, 2, wide), bf16),
            pltpu.VMEM((2, wide, depth), bf16),
            pltpu.VMEM((2, spread, wide), bf16),
        ]
    for slots in (ring, 2):
        for part in parts:
            scratch += [pltpu.VMEM((slots, 3, n, part.width), bf16) for n in part.route.sent]
    for _ in parts:
        scratch += [dma((count, 2)), dma((count, ring)), dma((count, 2)), dma((count, ring))]
    scratch += [dma((2, 3)), dma((2, 3)), dma((2,))]
    scratch += [
        pltpu.VMEM((2, sides, rank, rows), f32),
        pltpu.VMEM((2, peers, rank, rows), f32),
        pltpu.VMEM((2, 2, rank, rows), f32),
        dma, dma((2,)), dma((2, peers)), dma((2, peers)), dma((2, share)), dma((2, share)),
        dma((2, sides)), dma((2, sides)), dma((2, peers)), dma((2, peers)),
        dma((sides,)), dma((sides,)), dma((2, sides)), dma((2, sides)), dma((2,)),
    ]
    smem = pl.BlockSpec(memory_space=pltpu.SMEM)
    return pl.pallas_call(
        functools.partial(layer_kernel, axes, share, minor, parts, wide, chunks, keep_slots, ring),
        out_shape=[
            jax.ShapeDtypeStruct((rows, depth), bf16),
            jax.ShapeDtypeStruct((spread, rows), bf16),
            jax.ShapeDtypeStruct((in_count * rank, rows), bf16),
            jax.ShapeDtypeStruct((own_rows, depth), bf16),
            jax.ShapeDtypeStruct((own_rows, depth), bf16),
            jax.ShapeDtypeStruct((rows, hidden), bf16),
        ],
        in_specs=[smem] * 3 + [anywhere] * 6,
        out_specs=[anywhere] * 2 + [vmem] * 3 + [anywhere],
        scratch_shapes=scratch,
        compiler_params=pltpu.CompilerParams(
            collective_id=0, has_side_effects=True, vmem_limit_bytes=67043328
        ),
    )(lengths, adapters, table_row, tokens, grads, gate_up, down, in_table, table)


def adapter_kernel(grad_wide_t, tok, code_wide_t, up_grad, layer, inward, *outs):
    in_grad, out_grad, layer_out, inward_out = outs
    in_grad[...] = nn(grad_wide_t[...], tok[...]).astype(bf16)
    out_grad[...] = (adapter_scale * nn(code_wide_t[...], up_grad[...])).astype(bf16)
    layer_out[...] = layer[...]
    inward_out[...] = inward[...]


def adapter_call(grad_wide_t, tok, code_wide_t, up_grad, layer, inward):
    rows, depth = tok.shape
    hidden = up_grad.shape[1]
    spread, slots, own_rows = code_wide_t.shape[0], grad_wide_t.shape[0], layer.shape[0]
    steps = pieces if hidden % (pieces * lane) == 0 and own_rows % (pieces * 16) == 0 else 1
    by_rows = pl.BlockSpec((slots // steps, depth), lambda i: (i, 0))
    by_columns = pl.BlockSpec((spread, hidden // steps), lambda i: (0, i))
    own = pl.BlockSpec((own_rows // steps, depth), lambda i: (i, 0))
    return pl.pallas_call(
        adapter_kernel,
        grid=(steps,),
        out_shape=[
            jax.ShapeDtypeStruct((slots, depth), bf16),
            jax.ShapeDtypeStruct((spread, hidden), bf16),
            jax.ShapeDtypeStruct(layer.shape, bf16),
            jax.ShapeDtypeStruct(inward.shape, bf16),
        ],
        in_specs=[
            pl.BlockSpec((slots // steps, rows), lambda i: (i, 0)),
            pl.BlockSpec((rows, depth), lambda i: (0, 0)),
            pl.BlockSpec((spread, rows), lambda i: (0, 0)),
            pl.BlockSpec((rows, hidden // steps), lambda i: (0, i)),
            own,
            own,
        ],
        out_specs=[by_rows, by_columns, own, own],
        compiler_params=pltpu.CompilerParams(vmem_limit_bytes=67043328),
    )(grad_wide_t, tok, code_wide_t, up_grad, layer, inward)


def on_device(
    tokens,
    output_gradient,
    gate_up_weight,
    down_weight,
    adapter_input_factor,
    adapter_output_factor,
    request_token_rows,
    request_adapter,
    adapter_table_row,
):
    rank = adapter_input_factor.shape[1]
    hidden_portion, width = down_weight.shape
    in_rows = adapter_input_factor.shape[0]
    out_rows = adapter_output_factor.shape[0]
    out_table = adapter_output_factor.reshape(out_rows * rank, hidden_portion)
    token_cols, code_wide_t, grad_wide_t, layer_output, input_gradient, up_grad = layer_call(
        request_token_rows.T, request_adapter.T, adapter_table_row, tokens, output_gradient,
        gate_up_weight, down_weight, adapter_input_factor, out_table, ("dp", "tensor"),
    )
    adapter_input_gradient, adapter_output_gradient, layer_output, input_gradient = adapter_call(
        grad_wide_t, token_cols, code_wide_t, up_grad, layer_output, input_gradient
    )
    adapter_input_gradient = adapter_input_gradient.reshape(in_rows, rank, width)
    adapter_output_gradient = adapter_output_gradient.reshape(out_rows, rank, hidden_portion)
    return (layer_output, input_gradient, adapter_input_gradient, adapter_output_gradient)


def solution(mesh):
    in_specs = (
        P("dp", None),
        P("dp", None),
        P("dp", None, "tensor"),
        P("tensor", "dp"),
        P("tensor", None, "dp"),
        P("dp", None, "tensor"),
        P(),
        P(),
        P(),
    )
    out_specs = (
        P("tensor", "dp"),
        P("tensor", "dp"),
        P("tensor", None, "dp"),
        P("dp", None, "tensor"),
    )
    return jax.shard_map(
        on_device, mesh=mesh, in_specs=in_specs, out_specs=out_specs, check_vma=False
    )
```

```python
import functools

import jax
import jax.numpy as jnp
from jax import lax
from jax.experimental import pallas as pl
from jax.experimental.pallas import tpu as pltpu
from jax.sharding import PartitionSpec as P

adapter_scale = 0.5
lane = 128
pieces = 4
ends = (16, 16)
f32 = jnp.float32
bf16 = jnp.bfloat16


def bit_count(n):
    bits = n.bit_length() - 1
    assert n == 1 << bits
    return bits


def nn(x, y):
    return jnp.dot(x, y, preferred_element_type=f32)


def nt(x, y):
    return lax.dot_general(x, y, (((1,), (1,)), ((), ())), preferred_element_type=f32)


def both_of(*conds):
    conds = [cond for cond in conds if cond is not None]
    return functools.reduce(jnp.logical_and, conds) if conds else None


def run_if(cond, body):
    if cond is None:
        body()
    else:
        pl.when(cond)(body)


class Part:
    def __init__(self, route, base, width, first, last, chunks, inside):
        self.route, self.base, self.width = route, base, width
        self.first, self.last, self.inside = first, last, inside
        self.count = last - first if inside else chunks - (last - first)
        self.starts = (first == 0) == inside

    def holds(self, c):
        within = jnp.logical_and(c >= self.first, c < self.last)
        return within if self.inside else jnp.logical_not(within)

    def local(self, c):
        if self.inside:
            return c - self.first
        return jnp.where(c < self.first, c, c - (self.last - self.first))


class Route:
    def __init__(self, lines, rows):
        self.kinds, self.lines, self.sizes, self.sent, self.gives = [], [], [rows], [], []
        for line, length, give in lines:
            assert length in (2, 4)
            give = give and length == 4
            size = self.sizes[-1]
            kinds = ["chain"] * (length // 2 - 1) + ["swap"] + ["give"] * give
            after = {"chain": size, "swap": size // 2, "give": size // 4}
            for kind in kinds:
                self.kinds.append(kind)
                self.lines.append((line, length))
                self.gives.append(give)
                self.sizes.append(after[kind])
                self.sent.append(size - size // 4 if kind == "chain" and give else after[kind])
        self.count = len(self.kinds)

    def place(self, me, minor):
        self.active, self.low = [None], [0]
        self.peer, self.near, self.far, self.keep, self.cover = [], [], [], [], []
        for j in range(self.count):
            line, length = self.lines[j]
            pos = me % minor if line == 0 else me // minor
            step = 1 if line == 0 else minor
            upper = pos // (length // 2)
            active, low = self.active[-1], self.low[-1]
            inner = jnp.logical_or(pos == length // 2 - 1, pos == length // 2)
            outer = jnp.logical_not(inner)
            partner = me + (1 - 2 * (pos % 2)) * step
            self.keep.append(upper)
            self.cover.append(0)
            if self.kinds[j] == "chain":
                every, start = active, low
                self.near.append(both_of(active, inner))
                self.far.append(both_of(active, outer))
                self.peer.append(partner)
                self.active.append(both_of(active, inner))
                self.low.append(low)
                if self.gives[j]:
                    self.cover[-1] = low + (1 - upper) * (self.sizes[j] // 4)
                else:
                    self.cover[-1] = low
            elif self.kinds[j] == "swap":
                self.near.append(active)
                self.far.append(active)
                self.peer.append(me + (1 - 2 * upper) * step)
                self.active.append(active)
                self.low.append(low + upper * self.sizes[j + 1])
            else:
                self.near.append(both_of(every, outer))
                self.far.append(both_of(every, inner))
                self.peer.append(partner)
                self.active.append(every)
                self.low.append(start + pos * self.sizes[j + 1])
                self.cover[-1] = start + upper * 3 * self.sizes[j + 1]


def layer_kernel(axes, share, minor, parts, wide, chunks, keep_slots, ring, *refs):
    refs = list(refs)

    def take(count):
        taken, refs[:count] = refs[:count], []
        return taken

    lengths, adapters, table_row, tok_rows, grad_rows, gate_up, down, in_table, table = take(9)
    tok_out, code_out, grad_wide_t, layer_out, inward_out, up_out = take(6)
    tok, code_wide_t = take(2)
    layer, inward, grad, code, code_t, in_buf, slot_ref, which_ref = take(8)
    need_s, need_r, mine_ref, red32, red16_s, red16_r = take(6)
    x2, own, full, acc_t = take(4)
    w_f, d_f, t_f, w_b, d_b, t_b = take(6)
    routes = [part.route for part in parts]
    arrive = [take(route.count) for route in routes]
    leave = [take(route.count) for route in routes]
    sems = [take(4) for _ in parts]
    fwd_sem, bwd_sem, out_sem = take(3)
    sum_tensor, sum_dp, code_part = take(3)
    in_sem, own_sem, row_s, row_r, share_s, share_r, ten_s, ten_r, dp_s, dp_r = take(10)
    need_ss, need_rs, red_s, red_r, early_sem = take(5)
    axis, across = axes
    rows, depth = tok.shape
    group_rows = tok_rows.shape[0]
    in_count, rank = in_table.shape[:2]
    out_count = table.shape[0] // rank
    me = lax.axis_index(axis)
    peers = lax.axis_size(axis)
    side = lax.axis_index(across)
    sides = lax.axis_size(across)
    piece = depth // share
    own_rows = rows // sides
    requests = lengths.shape[0]
    needed = peers // sides * requests
    for route in routes:
        route.place(me, minor)

    barrier = pltpu.get_barrier_semaphore()
    for k in range(1, peers):
        pl.semaphore_signal(
            barrier, inc=1, device_id={axis: lax.rem(me + k, peers)},
            device_id_type=pl.DeviceIdType.MESH,
        )
    for k in range(1, sides):
        pl.semaphore_signal(
            barrier, inc=1, device_id={across: lax.rem(side + k, sides)},
            device_id_type=pl.DeviceIdType.MESH,
        )

    def columns(c):
        return pl.ds(pl.multiple_of(c * wide, wide), wide)

    def weight_copies(c, bufs, sem):
        slot = c % 2
        return [
            pltpu.make_async_copy(gate_up.at[:, :, columns(c)], bufs[0].at[slot], sem.at[slot, 0]),
            pltpu.make_async_copy(down.at[columns(c), :], bufs[1].at[slot], sem.at[slot, 1]),
            pltpu.make_async_copy(table.at[:, columns(c)], bufs[2].at[slot], sem.at[slot, 2]),
        ]

    def fetch_forward(c):
        for copy in weight_copies(c, (w_f, d_f, t_f), fwd_sem):
            copy.start()

    def fetch_backward(c):
        for copy in weight_copies(c, (w_b, d_b, t_b), bwd_sem):
            copy.start()

    def remote(src, dst, send_sem, recv_sem, peer, name=axis):
        return pltpu.make_async_remote_copy(
            src_ref=src, dst_ref=dst, send_sem=send_sem, recv_sem=recv_sem,
            device_id={name: peer}, device_id_type=pl.DeviceIdType.MESH,
        )

    sources, targets = (tok_rows, grad_rows), (tok, grad)

    def group_at(k):
        return pl.ds(pl.multiple_of(k * group_rows, group_rows), group_rows)

    def piece_at(k, base=0):
        return pl.ds(pl.multiple_of(base + k * piece, lane), piece)

    def row_copy(a, k, sent):
        peer = lax.rem(me + k, peers)
        owner = me if sent else peer
        part = side % share
        return remote(
            sources[a].at[:, piece_at(part, peer * depth)],
            targets[a].at[group_at(owner), piece_at(part)],
            row_s.at[a, k], row_r.at[a, owner], peer,
        )

    def own_copy(a):
        part = side % share
        return pltpu.make_async_copy(
            sources[a].at[:, piece_at(part, me * depth)],
            targets[a].at[group_at(me), piece_at(part)],
            own_sem.at[a],
        )

    def flip(k, bit):
        return k + bit * (1 - 2 * (k // bit % 2))

    share_steps, masks = [], [0]
    for level in range(bit_count(share) - 1, -1, -1):
        share_steps.append((1 << level, list(masks)))
        masks += [m ^ (1 << level) for m in masks]

    def share_copies(a, level, sent):
        bit, held = share_steps[level]
        copies = []
        for n, mask in enumerate(held):
            part = side % share
            for b in range(bit_count(share)):
                if (mask if sent else mask ^ bit) >> b & 1:
                    part = flip(part, 1 << b)
            at = targets[a].at[:, piece_at(part)]
            index = len(held) - 1 + n
            copies.append(
                remote(at, at, share_s.at[a, index], share_r.at[a, index], flip(side, bit), across)
            )
        return copies

    def code_copy(use, k, name, sent):
        if name == across:
            me_at, size, buf, send, recv = side, sides, sum_tensor, ten_s, ten_r
        else:
            me_at, size, buf, send, recv = me, peers, sum_dp, dp_s, dp_r
        peer = lax.rem(me_at + k, size)
        owner = me_at if sent else peer
        return remote(
            code_part.at[use, 0 if name == across else 1], buf.at[use, owner],
            send.at[use, k], recv.at[use, owner], peer, name,
        )

    def code_send(use, name, value):
        code_part[use, 0 if name == across else 1] = value
        for k in range(1, sides if name == across else peers):
            code_copy(use, k, name, True).start()

    def code_sum(use, name):
        size = sides if name == across else peers
        buf = sum_tensor if name == across else sum_dp
        me_at = side if name == across else me
        buf[use, me_at] = code_part[use, 0 if name == across else 1]
        for k in range(1, size):
            code_copy(use, k, name, False).wait_recv()
        value = buf[use, 0]
        for k in range(1, size):
            value = value + buf[use, k]
        return value

    def need_copy(k, sent):
        peer = lax.rem(side + k, sides)
        owner = side if sent else peer
        return remote(
            need_s.at[peer], need_r.at[owner], need_ss.at[k], need_rs.at[owner], peer, across
        )

    def other(mask):
        place = side
        for b in range(bit_count(sides)):
            if mask >> b & 1:
                place = flip(place, 1 << b)
        return place

    sums = (layer, inward)

    def block_of(a, mask):
        at = pl.ds(pl.multiple_of(other(mask) * own_rows, own_rows), own_rows)
        return sums[a].at[at, :]

    def masks_of(b):
        return [m for m in range(1, sides) if m & -m == 1 << b]

    later = [m for m in range(1, sides) if m % 2 == 0]

    def reduce_copy(a, mask):
        if mask % 2:
            source, target = block_of(a, mask), red32.at[a, mask // 2]
        else:
            source, target = [buf.at[a, later.index(mask)] for buf in (red16_s, red16_r)]
        return remote(
            source, target, red_s.at[a, mask], red_r.at[a, mask], flip(side, mask & -mask), across
        )

    def reduce_start(a, b):
        for mask in masks_of(b):
            if b:
                red16_s[a, later.index(mask)] = block_of(a, mask)[...].astype(bf16)
            reduce_copy(a, mask).start()

    def reduce_end(a, b):
        for mask in masks_of(b):
            reduce_copy(a, mask).wait_recv()
            more = red32[a, mask // 2] if b == 0 else red16_r[a, later.index(mask)].astype(f32)
            block_of(a, mask ^ (1 << b))[...] += more

    def folded(block, count, read):
        def add(i, carry):
            ids = lax.broadcasted_iota(jnp.int32, (block, rank, rows), 0) + i * block
            kept = jnp.where(ids == slot_here[None], read(i), 0.0)
            return carry + jnp.sum(kept, axis=0)

        return lax.fori_loop(0, count // block, add, jnp.zeros((rank, rows), f32))

    def widen(block, count, value, write):
        def put(i, carry):
            ids = lax.broadcasted_iota(jnp.int32, (block, rank, rows), 0) + i * block
            kept = jnp.where(ids == slot_here[None], value[None], 0.0)
            write(i, kept.reshape(block * rank, rows).astype(bf16))
            return carry

        lax.fori_loop(0, count // block, put, 0)

    spots = (0, 2, 1)

    def sum_copies(p, j, n):
        sum_s, sum_r = sems[p][:2]
        blocks = [pl.ds(0, 2), pl.ds(2, 1)] if j == 0 else [pl.ds(0, 3)]
        rows_of = [0, sum_s.shape[0] - 1] if j == 0 else [j]
        return [
            remote(
                leave[p][j].at[n % 2, block], arrive[p][j].at[n % ring, block],
                sum_s.at[k, n % 2], sum_r.at[k, n % ring], routes[p].peer[j],
            )
            for block, k in zip(blocks, rows_of)
        ]

    def first_hop(p, c, late):
        route, n = routes[p], parts[p].local(c)
        cols = pl.ds(parts[p].base, parts[p].width)
        size = route.sent[0]
        if route.kinds[0] == "chain":
            low = route.cover[0]
        else:
            low = (1 - route.keep[0]) * size

        def body():
            copy = sum_copies(p, 0, n)[late]
            pl.when(n >= 2)(lambda: copy.wait_send())
            for q in (1,) if late else (0, 2):
                value = own[c % keep_slots, q, pl.ds(align(low), size), cols]
                leave[p][0][n % 2, spots[q]] = value.astype(bf16)
            copy.start()

        run_if(route.far[0], body)

    def all_copy(p, m, c, n, mine):
        route, base, width = routes[p], parts[p].base, parts[p].width
        j = route.count - 1 - m
        all_s, all_r = sems[p][2:]
        size = route.sent[j]
        if route.kinds[j] == "chain":
            low = route.cover[j]
        elif mine:
            low = route.low[j + 1]
        elif route.kinds[j] == "give":
            low = route.cover[j]
        else:
            low = route.low[j] + (1 - route.keep[j]) * size
        at = full.at[c, :, pl.ds(align(low), size), pl.ds(base, width)]
        return remote(at, at, all_s.at[m, n % 2], all_r.at[m, n % ring], route.peer[j])

    def align(low):
        return low if isinstance(low, int) else pl.multiple_of(low, 16)

    def start_all(p, m, c):
        route, n = routes[p], parts[p].local(c)
        j = route.count - 1 - m

        def body():
            pl.when(n >= 2)(lambda: all_copy(p, m, c, n, True).wait_send())
            all_copy(p, m, c, n, True).start()

        run_if(route.near[j] if route.kinds[j] == "give" else None, body)
        if route.kinds[j] == "chain" and m + 1 < route.count:
            start_all(p, m + 1, c)

    def sum_task(p, t, c):
        route, n = routes[p], parts[p].local(c)
        cols = pl.ds(parts[p].base, parts[p].width)
        held = c % keep_slots

        if t == 0:
            pl.when(c > 0)(lambda: first_hop(p, c, 0))
            first_hop(p, c, 1)
            return
        fresh = route.kinds[t - 1] != "give"

        def total(q, low, skip, size):
            value = own[held, q, pl.ds(align(low), size), cols]
            if fresh:
                at = pl.ds(skip if isinstance(skip, int) else pl.multiple_of(skip, 16), size)
                value = value + arrive[p][t - 1][n % ring, spots[q], at, :].astype(f32)
            return value

        def ready():
            pl.when(n >= 2)(lambda: sum_copies(p, t, n)[0].wait_send())

        def send(low, skip, size):
            ready()
            for q in range(3):
                leave[p][t][n % 2, spots[q]] = total(q, low, skip, size).astype(bf16)
            sum_copies(p, t, n)[0].start()

        def stay(low, skip, size):
            if fresh:
                for q in range(3):
                    own[held, q, pl.ds(align(low), size), cols] = total(q, low, skip, size)

        def receive():
            for copy in sum_copies(p, t - 1, n):
                copy.wait_recv()

        def body():
            low, size = route.low[t], route.sizes[t]
            if fresh:
                receive()
            elif t:

                def back():
                    receive()
                    for q in range(3):
                        own[held, q, pl.ds(align(low), size), cols] += arrive[p][t - 1][
                            n % ring, spots[q]
                        ].astype(f32)

                run_if(route.near[t - 1], back)
            if t == route.count:
                gate_pre, up_pre, hidden_grad = [total(q, low, 0, size) for q in range(3)]
                sig = jax.nn.sigmoid(gate_pre)
                act_gate = gate_pre * sig
                at = pl.ds(align(low), size)
                full[c, 2, at, cols] = (act_gate * up_pre).astype(bf16)
                full[c, 1, at, cols] = (hidden_grad * act_gate).astype(bf16)
                full[c, 0, at, cols] = (
                    hidden_grad * up_pre * sig * (1.0 + gate_pre * (1.0 - sig))
                ).astype(bf16)
                start_all(p, 0, c)
                return
            side = route.keep[t]
            if route.kinds[t] == "chain":
                skip = route.cover[t] - low
                run_if(route.far[t], lambda: send(route.cover[t], skip, route.sent[t]))
                if fresh:
                    run_if(route.near[t], lambda: stay(low, 0, size))
                return
            half = size // 2
            if route.kinds[t] == "give":
                send(low + side * half, side * half, half)
                stay(low + (1 - side) * half, (1 - side) * half, half)
            elif t and route.kinds[t - 1] == "chain" and route.gives[t - 1]:
                quarter = half // 2
                send(low + (1 - side) * half, (1 - side) * quarter, half)
                stay(low + quarter + side * quarter, side * half, quarter)
            else:
                send(low + (1 - side) * half, (1 - side) * half, half)
                stay(low + side * half, side * half, half)

        run_if(route.active[t], body)

    def all_task(p, m, c):
        route = routes[p]
        j = route.count - 1 - m

        def body():
            all_copy(p, m, c, parts[p].local(c), False).wait_recv()
            if m + 1 < route.count:
                start_all(p, m + 1, c)

        run_if(route.active[j] if route.kinds[j] == "swap" else route.far[j], body)

    def tasks(p, it):
        route = routes[p]
        for t in range(2 * route.count, -1, -1):
            c = it - t

            def go(t=t, c=c):
                if t <= route.count:
                    sum_task(p, t, c)
                else:
                    all_task(p, t - route.count - 1, c)

            pl.when(both_of(c >= 0, c < chunks, parts[p].holds(c)))(go)

    def forward_inward(c):
        slot, held = c % 2, c % keep_slots
        gate_copy, _, table_copy = weight_copies(c, (w_f, d_f, t_f), fwd_sem)
        gate_copy.wait()
        pre = nn(x2[...], w_f.at[slot].reshape(2 * depth, wide)[...])
        own[held, 0] = pre[:rows]
        own[held, 1] = pre[rows:]

    def forward_hidden(c):
        slot, held = c % 2, c % keep_slots
        weight_copies(c, (w_f, d_f, t_f), fwd_sem)[1].wait()
        own[held, 2] = nt(grad[...], d_f[slot])

    def forward_lift(c):
        slot, held = c % 2, c % keep_slots
        weight_copies(c, (w_f, d_f, t_f), fwd_sem)[2].wait()
        own[held, 1] += adapter_scale * nn(code[...], t_f[slot])
        pl.when(c + 2 < chunks)(lambda: fetch_forward(c + 2))

    def forward(c):
        forward_inward(c)
        forward_hidden(c)
        forward_lift(c)

    def out_copy(c):
        return pltpu.make_async_copy(
            full.at[c, 1], up_out.at[:, columns(c)], out_sem.at[c % 2]
        )

    def backward_layer(c):
        slot = c % 2
        weight_copies(c, (w_b, d_b, t_b), bwd_sem)[1].wait()
        layer[...] += nn(full[c, 2], d_b[slot])

    def backward_code(c):
        weight_copies(c, (w_b, d_b, t_b), bwd_sem)[2].wait()
        code_t[...] += nt(t_b[c % 2], full[c, 1])

    def backward_inward(c):
        slot = c % 2
        pl.when(c >= 2)(lambda: out_copy(c - 2).wait())
        out_copy(c).start()
        weight_copies(c, (w_b, d_b, t_b), bwd_sem)[0].wait()
        grads = full[c, 0:2].reshape(2 * rows, wide)
        weights = w_b.at[slot].reshape(2 * depth, wide)
        block = min(512, 2 * depth)

        def add(i, carry):
            at = pl.ds(pl.multiple_of(i * block, block), block)
            more = nt(weights[at, :], grads)
            for k in range(2 * rows // lane):
                acc_t[k, at, :] += more[:, lane * k : lane * (k + 1)]
            return carry

        lax.fori_loop(0, 2 * depth // block, add, 0)
        pl.when(c + 2 < chunks)(lambda: fetch_backward(c + 2))

    def backward(c):
        backward_code(c)
        backward_layer(c)
        backward_inward(c)

    for c in range(min(2, chunks)):
        fetch_forward(c)
    in_copy = pltpu.make_async_copy(in_table, in_buf, in_sem)
    in_copy.start()
    for a in range(2):
        own_copy(a).start()
    pl.semaphore_wait(barrier, peers - 1 + sides - 1)
    for a in range(2):
        for k in range(1, peers):
            row_copy(a, k, True).start()
    spot = lax.broadcasted_iota(jnp.int32, (rank, rows), 1)
    slots = jnp.zeros((rank, rows), jnp.int32)
    which = jnp.zeros((rank, rows), jnp.int32)
    for k in range(peers):
        first = jnp.int32(k * group_rows)
        for q in range(lengths.shape[0]):
            last = first + lengths[q, k]
            inside = jnp.logical_and(spot >= first, spot < last)
            slots = jnp.where(inside, table_row[adapters[q, k]], slots)
            which = jnp.where(inside, k * requests + q, which)
            first = last
    slot_ref[...] = slots
    which_ref[...] = which
    acc_t[...] = jnp.zeros_like(acc_t)
    layer[...] = jnp.zeros_like(layer)
    code_t[...] = jnp.zeros_like(code_t)
    in_copy.wait()
    for s in range(sides):
        for i in range(needed):
            at = table_row[adapters[i % requests, s * (needed // requests) + i // requests]]
            at = at - side * in_count
            here = jnp.logical_and(at >= 0, at < in_count)
            row = in_buf[jnp.clip(at, 0, in_count - 1)].astype(f32)
            need_s[s, i] = jnp.where(here, row, 0.0).astype(bf16)
    hops = len(share_steps)

    def share_on(a, level):
        for copy in share_copies(a, level, False):
            copy.wait_recv()
        if level + 1 < hops:
            for copy in share_copies(a, level + 1, True):
                copy.start()

    for a in range(2):
        own_copy(a).wait()
        for k in range(1, peers):
            row_copy(a, k, False).wait_recv()
        if hops:
            for copy in share_copies(a, 0, True):
                copy.start()
    for level in range(hops):
        share_on(0, level)
    every = sides * needed
    some = nt(need_s[...].reshape(every * rank, depth), tok[...]).reshape(every, rank, rows)
    ids = lax.broadcasted_iota(jnp.int32, (every, rank, rows), 0)
    code_send(0, across, jnp.sum(jnp.where(ids == which_ref[...][None], some, 0.0), axis=0))
    for level in range(hops - 1):
        share_on(1, level)
    row = lax.broadcasted_iota(jnp.int32, (lane, 2 * lane), 0)
    column = lax.broadcasted_iota(jnp.int32, (lane, 2 * lane), 1)
    for g in range(2):
        pick = (column == 2 * row + g).astype(f32).astype(bf16)
        for k in range(depth // lane):
            x2[g * rows : (g + 1) * rows, 2 * lane * k : 2 * lane * (k + 1)] = nn(
                tok[:, lane * k : lane * (k + 1)], pick
            ).astype(bf16)
    code_send(0, axis, code_sum(0, across))
    forward_inward(0)
    if share_steps:
        for copy in share_copies(1, len(share_steps) - 1, False):
            copy.wait_recv()
    forward_hidden(0)
    for p, part in enumerate(parts):
        if part.starts:
            first_hop(p, jnp.int32(0), 0)
    for k in range(1, sides):
        need_copy(k, True).start()
    code_low = code_sum(0, axis).astype(bf16).astype(f32)
    slot_here = slot_ref[...] - me * out_count
    block = min(32, out_count)

    def put_code(i, value):
        code_wide_t[pl.ds(pl.multiple_of(i * block * rank, block * rank), block * rank), :] = value

    widen(block, out_count, code_low, put_code)
    code[...] = code_wide_t[...].T
    early = [
        pltpu.make_async_copy(tok, tok_out, early_sem.at[0]),
        pltpu.make_async_copy(code_wide_t, code_out, early_sem.at[1]),
    ]
    for copy in early:
        copy.start()
    forward_lift(0)
    for c in range(min(2, chunks)):
        fetch_backward(c)
    lag = 2 * max(route.count for route in routes)

    def step(it, carry):
        tasks(0, it)
        pl.when(it + 1 < chunks)(lambda: forward(it + 1))
        for p in range(1, len(parts)):
            tasks(p, it)
        pl.when(it >= lag)(lambda: backward(it - lag))
        return carry

    lax.fori_loop(0, chunks + lag - 1, step, 0)
    for p in range(len(parts)):
        tasks(p, jnp.int32(chunks + lag - 1))
    bits = bit_count(sides)
    backward_code(chunks - 1)
    slot_here = slot_ref[...] - me * out_count
    block = min(32, out_count)

    def out_codes(i):
        at = pl.ds(pl.multiple_of(i * block * rank, block * rank), block * rank)
        return code_t[at, :].reshape(block, rank, rows)

    code_send(1, across, folded(block, out_count, out_codes))
    backward_layer(chunks - 1)
    if bits:
        reduce_start(0, 0)
    backward_inward(chunks - 1)
    code_send(1, axis, code_sum(1, across))
    half = rows // lane
    for k in range(half):
        inward[lane * k : lane * (k + 1), :] = (
            acc_t.at[k][pl.ds(0, depth, stride=2), :]
            + acc_t.at[half + k][pl.ds(1, depth, stride=2), :]
        ).T
    if bits:
        reduce_start(1, 0)
    for b in range(bits - 1):
        for a in range(2):
            reduce_end(a, b)
            reduce_start(a, b + 1)
    for copy in early:
        copy.wait()
    need = need_s[side].astype(f32)
    for k in range(1, sides):
        need_copy(k, False).wait_recv()
        need = need + need_r[lax.rem(side + k, sides)].astype(f32)
    need = need.reshape(needed * rank, depth).astype(bf16)
    code_grad = (adapter_scale * code_sum(1, axis)).astype(bf16).astype(f32)
    ids = lax.broadcasted_iota(jnp.int32, (needed, rank, rows), 0) + side * needed
    mine = jnp.where(ids == which_ref[...][None], code_grad[None], 0.0)
    mine_ref[...] = mine.reshape(needed * rank, rows).T
    own_at = pl.ds(pl.multiple_of(side * own_rows, own_rows), own_rows)
    term = nn(mine_ref[own_at, :].astype(bf16), need)
    slot_here = slot_ref[...] - side * in_count
    block = min(32, in_count)

    def put_grad(i, value):
        grad_wide_t[pl.ds(pl.multiple_of(i * block * rank, block * rank), block * rank), :] = value

    widen(block, in_count, code_grad, put_grad)
    if bits:
        reduce_end(0, bits - 1)
    layer_out[...] = block_of(0, 0)[...].astype(bf16)
    if bits:
        reduce_end(1, bits - 1)
    inward_out[...] = (block_of(1, 0)[...] + term).astype(bf16)
    for k in range(1, sides):
        need_copy(k, True).wait_send()
    for a in range(2):
        for mask in range(1, sides):
            reduce_copy(a, mask).wait_send()
    for a in range(2):
        for k in range(1, peers):
            row_copy(a, k, True).wait_send()
        for level in range(len(share_steps)):
            for copy in share_copies(a, level, True):
                copy.wait_send()
    for use in range(2):
        for k in range(1, sides):
            code_copy(use, k, across, True).wait_send()
        for k in range(1, peers):
            code_copy(use, k, axis, True).wait_send()
    for c in range(max(chunks - 2, 0), chunks):
        out_copy(c).wait()
    for p, route in enumerate(routes):
        for n in range(max(parts[p].count - 2, 0), parts[p].count):
            for j in range(route.count):
                for copy in sum_copies(p, j, n):
                    run_if(route.far[j], copy.wait_send)
                m = route.count - 1 - j
                run_if(route.near[j], lambda: all_copy(p, m, 0, n, True).wait_send())


def layer_call(lengths, adapters, table_row, tokens, grads, gate_up, down, in_table, table, axes):
    hidden, depth = down.shape
    spread = table.shape[0]
    in_count, rank = in_table.shape[:2]
    peers, sides = [lax.axis_size(axis) for axis in axes]
    rows = peers * tokens.shape[0]
    share = min(sides, max(depth // lane, 1))
    bits = bit_count(peers)
    minor = 1 << (bits // 2)
    major = peers // minor
    two = hidden % (2 * lane) == 0
    wide = 2 * lane if two else lane
    chunks = hidden // wide
    lines = [(0, minor, False), (1, major, False)]
    turned = [(1, major, False), (0, minor, False)]
    parts = [Part(Route(lines, rows), 0, lane, 0, chunks, chunks, True)]
    if two:
        first, last = chunks * ends[0] // 100, chunks - chunks * ends[1] // 100
        parts.append(Part(Route(turned, rows), lane, lane, first, last, chunks, True))
        if parts[-1].count < chunks:
            parts.append(Part(Route(lines, rows), lane, lane, first, last, chunks, False))
    count = max(part.route.count for part in parts)
    keep_slots, ring = count + 2, 2 * count + 2
    vmem = pl.BlockSpec(memory_space=pltpu.VMEM)
    anywhere = pl.BlockSpec(memory_space=pl.ANY)
    dma = pltpu.SemaphoreType.DMA
    own_rows = rows // sides
    needed = peers // sides * lengths.shape[0]
    later = max(sides // 2 - 1, 1)
    scratch = [
        pltpu.VMEM((rows, depth), bf16),
        pltpu.VMEM((spread, rows), bf16),
        pltpu.VMEM((rows, depth), f32),
        pltpu.VMEM((rows, depth), f32),
        pltpu.VMEM((rows, depth), bf16),
        pltpu.VMEM((rows, spread), bf16),
        pltpu.VMEM((spread, rows), f32),
        pltpu.VMEM(in_table.shape, bf16),
        pltpu.VMEM((rank, rows), jnp.int32),
        pltpu.VMEM((rank, rows), jnp.int32),
        pltpu.VMEM((sides, needed, rank, depth), bf16),
        pltpu.VMEM((sides, needed, rank, depth), bf16),
        pltpu.VMEM((rows, needed * rank), f32),
        pltpu.VMEM((2, max(sides // 2, 1), own_rows, depth), f32),
        pltpu.VMEM((2, later, own_rows, depth), bf16),
        pltpu.VMEM((2, later, own_rows, depth), bf16),
        pltpu.VMEM((2 * rows, 2 * depth), bf16),
        pltpu.VMEM((keep_slots, 3, rows, wide), f32),
        pltpu.VMEM((chunks, 3, rows, wide), bf16),
        pltpu.VMEM((2 * rows // lane, 2 * depth, lane), f32),
    ]
    for _ in range(2):
        scratch += [
            pltpu.VMEM((2, depth, 2, wide), bf16),
            pltpu.VMEM((2, wide, depth), bf16),
            pltpu.VMEM((2, spread, wide), bf16),
        ]
    for slots in (ring, 2):
        for part in parts:
            scratch += [pltpu.VMEM((slots, 3, n, part.width), bf16) for n in part.route.sent]
    for _ in parts:
        scratch += [dma((count + 1, 2)), dma((count + 1, ring)), dma((count, 2)), dma((count, ring))]
    scratch += [dma((2, 3)), dma((2, 3)), dma((2,))]
    scratch += [
        pltpu.VMEM((2, sides, rank, rows), f32),
        pltpu.VMEM((2, peers, rank, rows), f32),
        pltpu.VMEM((2, 2, rank, rows), f32),
        dma, dma((2,)), dma((2, peers)), dma((2, peers)), dma((2, share)), dma((2, share)),
        dma((2, sides)), dma((2, sides)), dma((2, peers)), dma((2, peers)),
        dma((sides,)), dma((sides,)), dma((2, sides)), dma((2, sides)), dma((2,)),
    ]
    smem = pl.BlockSpec(memory_space=pltpu.SMEM)
    return pl.pallas_call(
        functools.partial(layer_kernel, axes, share, minor, parts, wide, chunks, keep_slots, ring),
        out_shape=[
            jax.ShapeDtypeStruct((rows, depth), bf16),
            jax.ShapeDtypeStruct((spread, rows), bf16),
            jax.ShapeDtypeStruct((in_count * rank, rows), bf16),
            jax.ShapeDtypeStruct((own_rows, depth), bf16),
            jax.ShapeDtypeStruct((own_rows, depth), bf16),
            jax.ShapeDtypeStruct((rows, hidden), bf16),
        ],
        in_specs=[smem] * 3 + [anywhere] * 6,
        out_specs=[anywhere] * 2 + [vmem] * 3 + [anywhere],
        scratch_shapes=scratch,
        compiler_params=pltpu.CompilerParams(
            collective_id=0, has_side_effects=True, vmem_limit_bytes=67043328
        ),
    )(lengths, adapters, table_row, tokens, grads, gate_up, down, in_table, table)


def adapter_kernel(grad_wide_t, tok, code_wide_t, up_grad, layer, inward, *outs):
    in_grad, out_grad, layer_out, inward_out = outs
    in_grad[...] = nn(grad_wide_t[...], tok[...]).astype(bf16)
    out_grad[...] = (adapter_scale * nn(code_wide_t[...], up_grad[...])).astype(bf16)
    layer_out[...] = layer[...]
    inward_out[...] = inward[...]


def adapter_call(grad_wide_t, tok, code_wide_t, up_grad, layer, inward):
    rows, depth = tok.shape
    hidden = up_grad.shape[1]
    spread, slots, own_rows = code_wide_t.shape[0], grad_wide_t.shape[0], layer.shape[0]
    steps = pieces if hidden % (pieces * lane) == 0 and own_rows % (pieces * 16) == 0 else 1
    by_rows = pl.BlockSpec((slots // steps, depth), lambda i: (i, 0))
    by_columns = pl.BlockSpec((spread, hidden // steps), lambda i: (0, i))
    own = pl.BlockSpec((own_rows // steps, depth), lambda i: (i, 0))
    return pl.pallas_call(
        adapter_kernel,
        grid=(steps,),
        out_shape=[
            jax.ShapeDtypeStruct((slots, depth), bf16),
            jax.ShapeDtypeStruct((spread, hidden), bf16),
            jax.ShapeDtypeStruct(layer.shape, bf16),
            jax.ShapeDtypeStruct(inward.shape, bf16),
        ],
        in_specs=[
            pl.BlockSpec((slots // steps, rows), lambda i: (i, 0)),
            pl.BlockSpec((rows, depth), lambda i: (0, 0)),
            pl.BlockSpec((spread, rows), lambda i: (0, 0)),
            pl.BlockSpec((rows, hidden // steps), lambda i: (0, i)),
            own,
            own,
        ],
        out_specs=[by_rows, by_columns, own, own],
        compiler_params=pltpu.CompilerParams(vmem_limit_bytes=67043328),
    )(grad_wide_t, tok, code_wide_t, up_grad, layer, inward)


def on_device(
    tokens,
    output_gradient,
    gate_up_weight,
    down_weight,
    adapter_input_factor,
    adapter_output_factor,
    request_token_rows,
    request_adapter,
    adapter_table_row,
):
    rank = adapter_input_factor.shape[1]
    hidden_portion, width = down_weight.shape
    in_rows = adapter_input_factor.shape[0]
    out_rows = adapter_output_factor.shape[0]
    out_table = adapter_output_factor.reshape(out_rows * rank, hidden_portion)
    token_cols, code_wide_t, grad_wide_t, layer_output, input_gradient, up_grad = layer_call(
        request_token_rows.T, request_adapter.T, adapter_table_row, tokens, output_gradient,
        gate_up_weight, down_weight, adapter_input_factor, out_table, ("dp", "tensor"),
    )
    adapter_input_gradient, adapter_output_gradient, layer_output, input_gradient = adapter_call(
        grad_wide_t, token_cols, code_wide_t, up_grad, layer_output, input_gradient
    )
    adapter_input_gradient = adapter_input_gradient.reshape(in_rows, rank, width)
    adapter_output_gradient = adapter_output_gradient.reshape(out_rows, rank, hidden_portion)
    return (layer_output, input_gradient, adapter_input_gradient, adapter_output_gradient)


def solution(mesh):
    in_specs = (
        P("dp", None),
        P("dp", None),
        P("dp", None, "tensor"),
        P("tensor", "dp"),
        P("tensor", None, "dp"),
        P("dp", None, "tensor"),
        P(),
        P(),
        P(),
    )
    out_specs = (
        P("tensor", "dp"),
        P("tensor", "dp"),
        P("tensor", None, "dp"),
        P("dp", None, "tensor"),
    )
    return jax.shard_map(
        on_device, mesh=mesh, in_specs=in_specs, out_specs=out_specs, check_vma=False
    )
```

```python
import functools

import jax
import jax.numpy as jnp
from jax import lax
from jax.experimental import pallas as pl
from jax.experimental.pallas import tpu as pltpu
from jax.sharding import PartitionSpec as P

adapter_scale = 0.5
lane = 128
pieces = 4
ends = (16, 16)
f32 = jnp.float32
bf16 = jnp.bfloat16


def bit_count(n):
    bits = n.bit_length() - 1
    assert n == 1 << bits
    return bits


def nn(x, y):
    return jnp.dot(x, y, preferred_element_type=f32)


def nt(x, y):
    return lax.dot_general(x, y, (((1,), (1,)), ((), ())), preferred_element_type=f32)


def both_of(*conds):
    conds = [cond for cond in conds if cond is not None]
    return functools.reduce(jnp.logical_and, conds) if conds else None


def run_if(cond, body):
    if cond is None:
        body()
    else:
        pl.when(cond)(body)


class Part:
    def __init__(self, route, base, width, first, last, chunks, inside):
        self.route, self.base, self.width = route, base, width
        self.first, self.last, self.inside = first, last, inside
        self.count = last - first if inside else chunks - (last - first)
        self.starts = (first == 0) == inside

    def holds(self, c):
        within = jnp.logical_and(c >= self.first, c < self.last)
        return within if self.inside else jnp.logical_not(within)

    def local(self, c):
        if self.inside:
            return c - self.first
        return jnp.where(c < self.first, c, c - (self.last - self.first))


class Route:
    def __init__(self, lines, rows):
        self.kinds, self.lines, self.sizes, self.sent, self.gives = [], [], [rows], [], []
        for line, length, give in lines:
            assert length in (2, 4)
            give = give and length == 4
            size = self.sizes[-1]
            kinds = ["chain"] * (length // 2 - 1) + ["swap"] + ["give"] * give
            after = {"chain": size, "swap": size // 2, "give": size // 4}
            for kind in kinds:
                self.kinds.append(kind)
                self.lines.append((line, length))
                self.gives.append(give)
                self.sizes.append(after[kind])
                self.sent.append(size - size // 4 if kind == "chain" and give else after[kind])
        self.count = len(self.kinds)

    def place(self, me, minor):
        self.active, self.low = [None], [0]
        self.peer, self.near, self.far, self.keep, self.cover = [], [], [], [], []
        for j in range(self.count):
            line, length = self.lines[j]
            pos = me % minor if line == 0 else me // minor
            step = 1 if line == 0 else minor
            upper = pos // (length // 2)
            active, low = self.active[-1], self.low[-1]
            inner = jnp.logical_or(pos == length // 2 - 1, pos == length // 2)
            outer = jnp.logical_not(inner)
            partner = me + (1 - 2 * (pos % 2)) * step
            self.keep.append(upper)
            self.cover.append(0)
            if self.kinds[j] == "chain":
                every, start = active, low
                self.near.append(both_of(active, inner))
                self.far.append(both_of(active, outer))
                self.peer.append(partner)
                self.active.append(both_of(active, inner))
                self.low.append(low)
                if self.gives[j]:
                    self.cover[-1] = low + (1 - upper) * (self.sizes[j] // 4)
                else:
                    self.cover[-1] = low
            elif self.kinds[j] == "swap":
                self.near.append(active)
                self.far.append(active)
                self.peer.append(me + (1 - 2 * upper) * step)
                self.active.append(active)
                self.low.append(low + upper * self.sizes[j + 1])
            else:
                self.near.append(both_of(every, outer))
                self.far.append(both_of(every, inner))
                self.peer.append(partner)
                self.active.append(every)
                self.low.append(start + pos * self.sizes[j + 1])
                self.cover[-1] = start + upper * 3 * self.sizes[j + 1]


def layer_kernel(axes, share, minor, parts, wide, chunks, keep_slots, ring, *refs):
    refs = list(refs)

    def take(count):
        taken, refs[:count] = refs[:count], []
        return taken

    lengths, adapters, table_row, tok_rows, grad_rows, gate_up, down, in_table, table = take(9)
    tok_out, code_out, grad_out, slot_ref, layer_out, inward_out, up_out = take(7)
    tok, code_wide_t = take(2)
    layer, inward, grad, code, code_t, in_buf, which_ref = take(7)
    need_s, need_r, mine_ref, red32, red16_s, red16_r = take(6)
    x2, own, full, acc_t = take(4)
    w_f, d_f, t_f, w_b, d_b, t_b = take(6)
    routes = [part.route for part in parts]
    arrive = [take(route.count) for route in routes]
    leave = [take(route.count) for route in routes]
    sems = [take(4) for _ in parts]
    fwd_sem, bwd_sem, out_sem = take(3)
    sum_tensor, sum_dp, code_part = take(3)
    in_sem, own_sem, row_s, row_r, share_s, share_r, ten_s, ten_r, dp_s, dp_r = take(10)
    need_ss, need_rs, red_s, red_r, early_sem = take(5)
    axis, across = axes
    rows, depth = tok.shape
    group_rows = tok_rows.shape[0]
    in_count, rank = in_table.shape[:2]
    out_count = table.shape[0] // rank
    me = lax.axis_index(axis)
    peers = lax.axis_size(axis)
    side = lax.axis_index(across)
    sides = lax.axis_size(across)
    piece = depth // share
    own_rows = rows // sides
    requests = lengths.shape[0]
    needed = peers // sides * requests
    for route in routes:
        route.place(me, minor)

    barrier = pltpu.get_barrier_semaphore()
    for k in range(1, peers):
        pl.semaphore_signal(
            barrier, inc=1, device_id={axis: lax.rem(me + k, peers)},
            device_id_type=pl.DeviceIdType.MESH,
        )
    for k in range(1, sides):
        pl.semaphore_signal(
            barrier, inc=1, device_id={across: lax.rem(side + k, sides)},
            device_id_type=pl.DeviceIdType.MESH,
        )

    def columns(c):
        return pl.ds(pl.multiple_of(c * wide, wide), wide)

    def weight_copies(c, bufs, sem):
        slot = c % 2
        return [
            pltpu.make_async_copy(gate_up.at[:, :, columns(c)], bufs[0].at[slot], sem.at[slot, 0]),
            pltpu.make_async_copy(down.at[columns(c), :], bufs[1].at[slot], sem.at[slot, 1]),
            pltpu.make_async_copy(table.at[:, columns(c)], bufs[2].at[slot], sem.at[slot, 2]),
        ]

    def fetch_forward(c):
        for copy in weight_copies(c, (w_f, d_f, t_f), fwd_sem):
            copy.start()

    def fetch_backward(c):
        for copy in weight_copies(c, (w_b, d_b, t_b), bwd_sem):
            copy.start()

    def remote(src, dst, send_sem, recv_sem, peer, name=axis):
        return pltpu.make_async_remote_copy(
            src_ref=src, dst_ref=dst, send_sem=send_sem, recv_sem=recv_sem,
            device_id={name: peer}, device_id_type=pl.DeviceIdType.MESH,
        )

    sources, targets = (tok_rows, grad_rows), (tok, grad)

    def group_at(k):
        return pl.ds(pl.multiple_of(k * group_rows, group_rows), group_rows)

    def piece_at(k, base=0):
        return pl.ds(pl.multiple_of(base + k * piece, lane), piece)

    def row_copy(a, k, sent):
        peer = lax.rem(me + k, peers)
        owner = me if sent else peer
        part = side % share
        return remote(
            sources[a].at[:, piece_at(part, peer * depth)],
            targets[a].at[group_at(owner), piece_at(part)],
            row_s.at[a, k], row_r.at[a, owner], peer,
        )

    def own_copy(a):
        part = side % share
        return pltpu.make_async_copy(
            sources[a].at[:, piece_at(part, me * depth)],
            targets[a].at[group_at(me), piece_at(part)],
            own_sem.at[a],
        )

    def flip(k, bit):
        return k + bit * (1 - 2 * (k // bit % 2))

    share_steps, masks = [], [0]
    for level in range(bit_count(share) - 1, -1, -1):
        share_steps.append((1 << level, list(masks)))
        masks += [m ^ (1 << level) for m in masks]

    def share_copies(a, level, sent):
        bit, held = share_steps[level]
        copies = []
        for n, mask in enumerate(held):
            part = side % share
            for b in range(bit_count(share)):
                if (mask if sent else mask ^ bit) >> b & 1:
                    part = flip(part, 1 << b)
            at = targets[a].at[:, piece_at(part)]
            index = len(held) - 1 + n
            copies.append(
                remote(at, at, share_s.at[a, index], share_r.at[a, index], flip(side, bit), across)
            )
        return copies

    def code_copy(use, k, name, sent):
        if name == across:
            me_at, size, buf, send, recv = side, sides, sum_tensor, ten_s, ten_r
        else:
            me_at, size, buf, send, recv = me, peers, sum_dp, dp_s, dp_r
        peer = lax.rem(me_at + k, size)
        owner = me_at if sent else peer
        return remote(
            code_part.at[use, 0 if name == across else 1], buf.at[use, owner],
            send.at[use, k], recv.at[use, owner], peer, name,
        )

    def code_send(use, name, value):
        code_part[use, 0 if name == across else 1] = value
        for k in range(1, sides if name == across else peers):
            code_copy(use, k, name, True).start()

    def code_sum(use, name):
        size = sides if name == across else peers
        buf = sum_tensor if name == across else sum_dp
        me_at = side if name == across else me
        buf[use, me_at] = code_part[use, 0 if name == across else 1]
        for k in range(1, size):
            code_copy(use, k, name, False).wait_recv()
        value = buf[use, 0]
        for k in range(1, size):
            value = value + buf[use, k]
        return value

    def need_copy(k, sent):
        peer = lax.rem(side + k, sides)
        owner = side if sent else peer
        return remote(
            need_s.at[peer], need_r.at[owner], need_ss.at[k], need_rs.at[owner], peer, across
        )

    def other(mask):
        place = side
        for b in range(bit_count(sides)):
            if mask >> b & 1:
                place = flip(place, 1 << b)
        return place

    sums = (layer, inward)

    def block_of(a, mask):
        at = pl.ds(pl.multiple_of(other(mask) * own_rows, own_rows), own_rows)
        return sums[a].at[at, :]

    def masks_of(b):
        return [m for m in range(1, sides) if m & -m == 1 << b]

    later = [m for m in range(1, sides) if m % 2 == 0]

    def reduce_copy(a, mask):
        if mask % 2:
            source, target = block_of(a, mask), red32.at[a, mask // 2]
        else:
            source, target = [buf.at[a, later.index(mask)] for buf in (red16_s, red16_r)]
        return remote(
            source, target, red_s.at[a, mask], red_r.at[a, mask], flip(side, mask & -mask), across
        )

    def reduce_start(a, b):
        for mask in masks_of(b):
            if b:
                red16_s[a, later.index(mask)] = block_of(a, mask)[...].astype(bf16)
            reduce_copy(a, mask).start()

    def reduce_end(a, b):
        for mask in masks_of(b):
            reduce_copy(a, mask).wait_recv()
            more = red32[a, mask // 2] if b == 0 else red16_r[a, later.index(mask)].astype(f32)
            block_of(a, mask ^ (1 << b))[...] += more

    def folded(block, count, read):
        def add(i, carry):
            ids = lax.broadcasted_iota(jnp.int32, (block, rank, rows), 0) + i * block
            kept = jnp.where(ids == slot_here[None], read(i), 0.0)
            return carry + jnp.sum(kept, axis=0)

        return lax.fori_loop(0, count // block, add, jnp.zeros((rank, rows), f32))

    def widen(block, count, value, write):
        def put(i, carry):
            ids = lax.broadcasted_iota(jnp.int32, (block, rank, rows), 0) + i * block
            kept = jnp.where(ids == slot_here[None], value[None], 0.0)
            write(i, kept.reshape(block * rank, rows).astype(bf16))
            return carry

        lax.fori_loop(0, count // block, put, 0)

    spots = (0, 2, 1)

    def sum_copies(p, j, n):
        sum_s, sum_r = sems[p][:2]
        blocks = [pl.ds(0, 2), pl.ds(2, 1)] if j == 0 else [pl.ds(0, 3)]
        rows_of = [0, sum_s.shape[0] - 1] if j == 0 else [j]
        return [
            remote(
                leave[p][j].at[n % 2, block], arrive[p][j].at[n % ring, block],
                sum_s.at[k, n % 2], sum_r.at[k, n % ring], routes[p].peer[j],
            )
            for block, k in zip(blocks, rows_of)
        ]

    def first_hop(p, c, late):
        route, n = routes[p], parts[p].local(c)
        cols = pl.ds(parts[p].base, parts[p].width)
        size = route.sent[0]
        if route.kinds[0] == "chain":
            low = route.cover[0]
        else:
            low = (1 - route.keep[0]) * size

        def body():
            copy = sum_copies(p, 0, n)[late]
            pl.when(n >= 2)(lambda: copy.wait_send())
            for q in (1,) if late else (0, 2):
                value = own[c % keep_slots, q, pl.ds(align(low), size), cols]
                leave[p][0][n % 2, spots[q]] = value.astype(bf16)
            copy.start()

        run_if(route.far[0], body)

    def all_copy(p, m, c, n, mine):
        route, base, width = routes[p], parts[p].base, parts[p].width
        j = route.count - 1 - m
        all_s, all_r = sems[p][2:]
        size = route.sent[j]
        if route.kinds[j] == "chain":
            low = route.cover[j]
        elif mine:
            low = route.low[j + 1]
        elif route.kinds[j] == "give":
            low = route.cover[j]
        else:
            low = route.low[j] + (1 - route.keep[j]) * size
        at = full.at[c, :, pl.ds(align(low), size), pl.ds(base, width)]
        return remote(at, at, all_s.at[m, n % 2], all_r.at[m, n % ring], route.peer[j])

    def align(low):
        return low if isinstance(low, int) else pl.multiple_of(low, 16)

    def start_all(p, m, c):
        route, n = routes[p], parts[p].local(c)
        j = route.count - 1 - m

        def body():
            pl.when(n >= 2)(lambda: all_copy(p, m, c, n, True).wait_send())
            all_copy(p, m, c, n, True).start()

        run_if(route.near[j] if route.kinds[j] == "give" else None, body)
        if route.kinds[j] == "chain" and m + 1 < route.count:
            start_all(p, m + 1, c)

    def sum_task(p, t, c):
        route, n = routes[p], parts[p].local(c)
        cols = pl.ds(parts[p].base, parts[p].width)
        held = c % keep_slots

        if t == 0:
            pl.when(c > 0)(lambda: first_hop(p, c, 0))
            first_hop(p, c, 1)
            return
        fresh = route.kinds[t - 1] != "give"

        def total(q, low, skip, size):
            value = own[held, q, pl.ds(align(low), size), cols]
            if fresh:
                at = pl.ds(skip if isinstance(skip, int) else pl.multiple_of(skip, 16), size)
                value = value + arrive[p][t - 1][n % ring, spots[q], at, :].astype(f32)
            return value

        def ready():
            pl.when(n >= 2)(lambda: sum_copies(p, t, n)[0].wait_send())

        def send(low, skip, size):
            ready()
            for q in range(3):
                leave[p][t][n % 2, spots[q]] = total(q, low, skip, size).astype(bf16)
            sum_copies(p, t, n)[0].start()

        def stay(low, skip, size):
            if fresh:
                for q in range(3):
                    own[held, q, pl.ds(align(low), size), cols] = total(q, low, skip, size)

        def receive():
            for copy in sum_copies(p, t - 1, n):
                copy.wait_recv()

        def body():
            low, size = route.low[t], route.sizes[t]
            if fresh:
                receive()
            elif t:

                def back():
                    receive()
                    for q in range(3):
                        own[held, q, pl.ds(align(low), size), cols] += arrive[p][t - 1][
                            n % ring, spots[q]
                        ].astype(f32)

                run_if(route.near[t - 1], back)
            if t == route.count:
                gate_pre, up_pre, hidden_grad = [total(q, low, 0, size) for q in range(3)]
                sig = jax.nn.sigmoid(gate_pre)
                act_gate = gate_pre * sig
                at = pl.ds(align(low), size)
                full[c, 2, at, cols] = (act_gate * up_pre).astype(bf16)
                full[c, 1, at, cols] = (hidden_grad * act_gate).astype(bf16)
                full[c, 0, at, cols] = (
                    hidden_grad * up_pre * sig * (1.0 + gate_pre * (1.0 - sig))
                ).astype(bf16)
                start_all(p, 0, c)
                return
            side = route.keep[t]
            if route.kinds[t] == "chain":
                skip = route.cover[t] - low
                run_if(route.far[t], lambda: send(route.cover[t], skip, route.sent[t]))
                if fresh:
                    run_if(route.near[t], lambda: stay(low, 0, size))
                return
            half = size // 2
            if route.kinds[t] == "give":
                send(low + side * half, side * half, half)
                stay(low + (1 - side) * half, (1 - side) * half, half)
            elif t and route.kinds[t - 1] == "chain" and route.gives[t - 1]:
                quarter = half // 2
                send(low + (1 - side) * half, (1 - side) * quarter, half)
                stay(low + quarter + side * quarter, side * half, quarter)
            else:
                send(low + (1 - side) * half, (1 - side) * half, half)
                stay(low + side * half, side * half, half)

        run_if(route.active[t], body)

    def all_task(p, m, c):
        route = routes[p]
        j = route.count - 1 - m

        def body():
            all_copy(p, m, c, parts[p].local(c), False).wait_recv()
            if m + 1 < route.count:
                start_all(p, m + 1, c)

        run_if(route.active[j] if route.kinds[j] == "swap" else route.far[j], body)

    def tasks(p, it):
        route = routes[p]
        for t in range(2 * route.count, -1, -1):
            c = it - t

            def go(t=t, c=c):
                if t <= route.count:
                    sum_task(p, t, c)
                else:
                    all_task(p, t - route.count - 1, c)

            pl.when(both_of(c >= 0, c < chunks, parts[p].holds(c)))(go)

    def forward_inward(c):
        slot, held = c % 2, c % keep_slots
        gate_copy, _, table_copy = weight_copies(c, (w_f, d_f, t_f), fwd_sem)
        gate_copy.wait()
        pre = nn(x2[...], w_f.at[slot].reshape(2 * depth, wide)[...])
        own[held, 0] = pre[:rows]
        own[held, 1] = pre[rows:]

    def forward_hidden(c):
        slot, held = c % 2, c % keep_slots
        weight_copies(c, (w_f, d_f, t_f), fwd_sem)[1].wait()
        own[held, 2] = nt(grad[...], d_f[slot])

    def forward_lift(c):
        slot, held = c % 2, c % keep_slots
        weight_copies(c, (w_f, d_f, t_f), fwd_sem)[2].wait()
        own[held, 1] += adapter_scale * nn(code[...], t_f[slot])
        pl.when(c + 2 < chunks)(lambda: fetch_forward(c + 2))

    def forward(c):
        forward_inward(c)
        forward_hidden(c)
        forward_lift(c)

    def out_copy(c):
        return pltpu.make_async_copy(
            full.at[c, 1], up_out.at[:, columns(c)], out_sem.at[c % 2]
        )

    def backward_layer(c):
        slot = c % 2
        weight_copies(c, (w_b, d_b, t_b), bwd_sem)[1].wait()
        layer[...] += nn(full[c, 2], d_b[slot])

    def backward_code(c):
        weight_copies(c, (w_b, d_b, t_b), bwd_sem)[2].wait()
        code_t[...] += nt(t_b[c % 2], full[c, 1])

    def backward_inward(c):
        slot = c % 2
        pl.when(c >= 2)(lambda: out_copy(c - 2).wait())
        out_copy(c).start()
        weight_copies(c, (w_b, d_b, t_b), bwd_sem)[0].wait()
        grads = full[c, 0:2].reshape(2 * rows, wide)
        weights = w_b.at[slot].reshape(2 * depth, wide)
        block = min(512, 2 * depth)

        def add(i, carry):
            at = pl.ds(pl.multiple_of(i * block, block), block)
            more = nt(weights[at, :], grads)
            for k in range(2 * rows // lane):
                acc_t[k, at, :] += more[:, lane * k : lane * (k + 1)]
            return carry

        lax.fori_loop(0, 2 * depth // block, add, 0)
        pl.when(c + 2 < chunks)(lambda: fetch_backward(c + 2))

    def backward(c):
        backward_code(c)
        backward_layer(c)
        backward_inward(c)

    for c in range(min(2, chunks)):
        fetch_forward(c)
    in_copy = pltpu.make_async_copy(in_table, in_buf, in_sem)
    in_copy.start()
    for a in range(2):
        own_copy(a).start()
    pl.semaphore_wait(barrier, peers - 1 + sides - 1)
    for a in range(2):
        for k in range(1, peers):
            row_copy(a, k, True).start()
    spot = lax.broadcasted_iota(jnp.int32, (rank, rows), 1)
    slots = jnp.zeros((rank, rows), jnp.int32)
    which = jnp.zeros((rank, rows), jnp.int32)
    for k in range(peers):
        first = jnp.int32(k * group_rows)
        for q in range(lengths.shape[0]):
            last = first + lengths[q, k]
            inside = jnp.logical_and(spot >= first, spot < last)
            slots = jnp.where(inside, table_row[adapters[q, k]], slots)
            which = jnp.where(inside, k * requests + q, which)
            first = last
    slot_ref[...] = slots
    which_ref[...] = which
    acc_t[...] = jnp.zeros_like(acc_t)
    layer[...] = jnp.zeros_like(layer)
    code_t[...] = jnp.zeros_like(code_t)
    in_copy.wait()
    for s in range(sides):
        for i in range(needed):
            at = table_row[adapters[i % requests, s * (needed // requests) + i // requests]]
            at = at - side * in_count
            here = jnp.logical_and(at >= 0, at < in_count)
            row = in_buf[jnp.clip(at, 0, in_count - 1)].astype(f32)
            need_s[s, i] = jnp.where(here, row, 0.0).astype(bf16)
    hops = len(share_steps)

    def share_on(a, level):
        for copy in share_copies(a, level, False):
            copy.wait_recv()
        if level + 1 < hops:
            for copy in share_copies(a, level + 1, True):
                copy.start()

    for a in range(2):
        own_copy(a).wait()
        for k in range(1, peers):
            row_copy(a, k, False).wait_recv()
        if hops:
            for copy in share_copies(a, 0, True):
                copy.start()
    for level in range(hops):
        share_on(0, level)
    every = sides * needed
    some = nt(need_s[...].reshape(every * rank, depth), tok[...]).reshape(every, rank, rows)
    ids = lax.broadcasted_iota(jnp.int32, (every, rank, rows), 0)
    code_send(0, across, jnp.sum(jnp.where(ids == which_ref[...][None], some, 0.0), axis=0))
    for level in range(hops - 1):
        share_on(1, level)
    row = lax.broadcasted_iota(jnp.int32, (lane, 2 * lane), 0)
    column = lax.broadcasted_iota(jnp.int32, (lane, 2 * lane), 1)
    for g in range(2):
        pick = (column == 2 * row + g).astype(f32).astype(bf16)
        for k in range(depth // lane):
            x2[g * rows : (g + 1) * rows, 2 * lane * k : 2 * lane * (k + 1)] = nn(
                tok[:, lane * k : lane * (k + 1)], pick
            ).astype(bf16)
    code_send(0, axis, code_sum(0, across))
    forward_inward(0)
    if share_steps:
        for copy in share_copies(1, len(share_steps) - 1, False):
            copy.wait_recv()
    forward_hidden(0)
    for p, part in enumerate(parts):
        if part.starts:
            first_hop(p, jnp.int32(0), 0)
    for k in range(1, sides):
        need_copy(k, True).start()
    code_low = code_sum(0, axis).astype(bf16).astype(f32)
    slot_here = slot_ref[...] - me * out_count
    block = min(32, out_count)

    def put_code(i, value):
        code_wide_t[pl.ds(pl.multiple_of(i * block * rank, block * rank), block * rank), :] = value

    widen(block, out_count, code_low, put_code)
    code[...] = code_wide_t[...].T
    early = [
        pltpu.make_async_copy(tok, tok_out, early_sem.at[0]),
        pltpu.make_async_copy(code_wide_t, code_out, early_sem.at[1]),
    ]
    for copy in early:
        copy.start()
    forward_lift(0)
    for c in range(min(2, chunks)):
        fetch_backward(c)
    lag = 2 * max(route.count for route in routes)

    def step(it, carry):
        tasks(0, it)
        pl.when(it + 1 < chunks)(lambda: forward(it + 1))
        for p in range(1, len(parts)):
            tasks(p, it)
        pl.when(it >= lag)(lambda: backward(it - lag))
        return carry

    lax.fori_loop(0, chunks + lag - 1, step, 0)
    for p in range(len(parts)):
        tasks(p, jnp.int32(chunks + lag - 1))
    bits = bit_count(sides)
    backward_code(chunks - 1)
    slot_here = slot_ref[...] - me * out_count
    block = min(32, out_count)

    def out_codes(i):
        at = pl.ds(pl.multiple_of(i * block * rank, block * rank), block * rank)
        return code_t[at, :].reshape(block, rank, rows)

    code_send(1, across, folded(block, out_count, out_codes))
    backward_layer(chunks - 1)
    if bits:
        reduce_start(0, 0)
    backward_inward(chunks - 1)
    code_send(1, axis, code_sum(1, across))
    half = rows // lane
    for k in range(half):
        inward[lane * k : lane * (k + 1), :] = (
            acc_t.at[k][pl.ds(0, depth, stride=2), :]
            + acc_t.at[half + k][pl.ds(1, depth, stride=2), :]
        ).T
    if bits:
        reduce_start(1, 0)
    for b in range(bits - 1):
        for a in range(2):
            reduce_end(a, b)
            reduce_start(a, b + 1)
    for copy in early:
        copy.wait()
    need = need_s[side].astype(f32)
    for k in range(1, sides):
        need_copy(k, False).wait_recv()
        need = need + need_r[lax.rem(side + k, sides)].astype(f32)
    need = need.reshape(needed * rank, depth).astype(bf16)
    code_grad = (adapter_scale * code_sum(1, axis)).astype(bf16).astype(f32)
    ids = lax.broadcasted_iota(jnp.int32, (needed, rank, rows), 0) + side * needed
    mine = jnp.where(ids == which_ref[...][None], code_grad[None], 0.0)
    mine_ref[...] = mine.reshape(needed * rank, rows).T
    own_at = pl.ds(pl.multiple_of(side * own_rows, own_rows), own_rows)
    term = nn(mine_ref[own_at, :].astype(bf16), need)
    grad_out[...] = code_grad
    if bits:
        reduce_end(0, bits - 1)
    layer_out[...] = block_of(0, 0)[...].astype(bf16)
    if bits:
        reduce_end(1, bits - 1)
    inward_out[...] = (block_of(1, 0)[...] + term).astype(bf16)
    for k in range(1, sides):
        need_copy(k, True).wait_send()
    for a in range(2):
        for mask in range(1, sides):
            reduce_copy(a, mask).wait_send()
    for a in range(2):
        for k in range(1, peers):
            row_copy(a, k, True).wait_send()
        for level in range(len(share_steps)):
            for copy in share_copies(a, level, True):
                copy.wait_send()
    for use in range(2):
        for k in range(1, sides):
            code_copy(use, k, across, True).wait_send()
        for k in range(1, peers):
            code_copy(use, k, axis, True).wait_send()
    for c in range(max(chunks - 2, 0), chunks):
        out_copy(c).wait()
    for p, route in enumerate(routes):
        for n in range(max(parts[p].count - 2, 0), parts[p].count):
            for j in range(route.count):
                for copy in sum_copies(p, j, n):
                    run_if(route.far[j], copy.wait_send)
                m = route.count - 1 - j
                run_if(route.near[j], lambda: all_copy(p, m, 0, n, True).wait_send())


def layer_call(lengths, adapters, table_row, tokens, grads, gate_up, down, in_table, table, axes):
    hidden, depth = down.shape
    spread = table.shape[0]
    in_count, rank = in_table.shape[:2]
    peers, sides = [lax.axis_size(axis) for axis in axes]
    rows = peers * tokens.shape[0]
    share = min(sides, max(depth // lane, 1))
    bits = bit_count(peers)
    minor = 1 << (bits // 2)
    major = peers // minor
    two = hidden % (2 * lane) == 0
    wide = 2 * lane if two else lane
    chunks = hidden // wide
    lines = [(0, minor, False), (1, major, False)]
    turned = [(1, major, False), (0, minor, False)]
    parts = [Part(Route(lines, rows), 0, lane, 0, chunks, chunks, True)]
    if two:
        first, last = chunks * ends[0] // 100, chunks - chunks * ends[1] // 100
        parts.append(Part(Route(turned, rows), lane, lane, first, last, chunks, True))
        if parts[-1].count < chunks:
            parts.append(Part(Route(lines, rows), lane, lane, first, last, chunks, False))
    count = max(part.route.count for part in parts)
    keep_slots, ring = count + 2, 2 * count + 2
    vmem = pl.BlockSpec(memory_space=pltpu.VMEM)
    anywhere = pl.BlockSpec(memory_space=pl.ANY)
    dma = pltpu.SemaphoreType.DMA
    own_rows = rows // sides
    needed = peers // sides * lengths.shape[0]
    later = max(sides // 2 - 1, 1)
    scratch = [
        pltpu.VMEM((rows, depth), bf16),
        pltpu.VMEM((spread, rows), bf16),
        pltpu.VMEM((rows, depth), f32),
        pltpu.VMEM((rows, depth), f32),
        pltpu.VMEM((rows, depth), bf16),
        pltpu.VMEM((rows, spread), bf16),
        pltpu.VMEM((spread, rows), f32),
        pltpu.VMEM(in_table.shape, bf16),
        pltpu.VMEM((rank, rows), jnp.int32),
        pltpu.VMEM((sides, needed, rank, depth), bf16),
        pltpu.VMEM((sides, needed, rank, depth), bf16),
        pltpu.VMEM((rows, needed * rank), f32),
        pltpu.VMEM((2, max(sides // 2, 1), own_rows, depth), f32),
        pltpu.VMEM((2, later, own_rows, depth), bf16),
        pltpu.VMEM((2, later, own_rows, depth), bf16),
        pltpu.VMEM((2 * rows, 2 * depth), bf16),
        pltpu.VMEM((keep_slots, 3, rows, wide), f32),
        pltpu.VMEM((chunks, 3, rows, wide), bf16),
        pltpu.VMEM((2 * rows // lane, 2 * depth, lane), f32),
    ]
    for _ in range(2):
        scratch += [
            pltpu.VMEM((2, depth, 2, wide), bf16),
            pltpu.VMEM((2, wide, depth), bf16),
            pltpu.VMEM((2, spread, wide), bf16),
        ]
    for slots in (ring, 2):
        for part in parts:
            scratch += [pltpu.VMEM((slots, 3, n, part.width), bf16) for n in part.route.sent]
    for _ in parts:
        scratch += [dma((count + 1, 2)), dma((count + 1, ring)), dma((count, 2)), dma((count, ring))]
    scratch += [dma((2, 3)), dma((2, 3)), dma((2,))]
    scratch += [
        pltpu.VMEM((2, sides, rank, rows), f32),
        pltpu.VMEM((2, peers, rank, rows), f32),
        pltpu.VMEM((2, 2, rank, rows), f32),
        dma, dma((2,)), dma((2, peers)), dma((2, peers)), dma((2, share)), dma((2, share)),
        dma((2, sides)), dma((2, sides)), dma((2, peers)), dma((2, peers)),
        dma((sides,)), dma((sides,)), dma((2, sides)), dma((2, sides)), dma((2,)),
    ]
    smem = pl.BlockSpec(memory_space=pltpu.SMEM)
    return pl.pallas_call(
        functools.partial(layer_kernel, axes, share, minor, parts, wide, chunks, keep_slots, ring),
        out_shape=[
            jax.ShapeDtypeStruct((rows, depth), bf16),
            jax.ShapeDtypeStruct((spread, rows), bf16),
            jax.ShapeDtypeStruct((rank, rows), f32),
            jax.ShapeDtypeStruct((rank, rows), jnp.int32),
            jax.ShapeDtypeStruct((own_rows, depth), bf16),
            jax.ShapeDtypeStruct((own_rows, depth), bf16),
            jax.ShapeDtypeStruct((rows, hidden), bf16),
        ],
        in_specs=[smem] * 3 + [anywhere] * 6,
        out_specs=[anywhere] * 2 + [vmem] * 4 + [anywhere],
        scratch_shapes=scratch,
        compiler_params=pltpu.CompilerParams(
            collective_id=0, has_side_effects=True, vmem_limit_bytes=67043328
        ),
    )(lengths, adapters, table_row, tokens, grads, gate_up, down, in_table, table)


def adapter_kernel(across, code_grad, slots, tok, code_wide_t, up_grad, layer, inward, *outs):
    in_grad, out_grad, layer_out, inward_out = outs
    rank, rows = code_grad.shape
    block = in_grad.shape[0] // rank
    first = (lax.axis_index(across) * pl.num_programs(0) + pl.program_id(0)) * block
    ids = lax.broadcasted_iota(jnp.int32, (block, rank, rows), 0) + first
    wide = jnp.where(ids == slots[...][None], code_grad[...][None], 0.0)
    wide = wide.reshape(block * rank, rows).astype(bf16)
    in_grad[...] = nn(wide, tok[...]).astype(bf16)
    out_grad[...] = (adapter_scale * nn(code_wide_t[...], up_grad[...])).astype(bf16)
    layer_out[...] = layer[...]
    inward_out[...] = inward[...]


def adapter_call(code_grad, slot_of, in_count, across, tok, code_wide_t, up_grad, layer, inward):
    rows, depth = tok.shape
    hidden = up_grad.shape[1]
    rank = code_grad.shape[0]
    spread, slots, own_rows = code_wide_t.shape[0], in_count * rank, layer.shape[0]
    steps = pieces if hidden % (pieces * lane) == 0 and own_rows % (pieces * 16) == 0 else 1
    by_rows = pl.BlockSpec((slots // steps, depth), lambda i: (i, 0))
    by_columns = pl.BlockSpec((spread, hidden // steps), lambda i: (0, i))
    own = pl.BlockSpec((own_rows // steps, depth), lambda i: (i, 0))
    return pl.pallas_call(
        functools.partial(adapter_kernel, across),
        grid=(steps,),
        out_shape=[
            jax.ShapeDtypeStruct((slots, depth), bf16),
            jax.ShapeDtypeStruct((spread, hidden), bf16),
            jax.ShapeDtypeStruct(layer.shape, bf16),
            jax.ShapeDtypeStruct(inward.shape, bf16),
        ],
        in_specs=[
            pl.BlockSpec((rank, rows), lambda i: (0, 0)),
            pl.BlockSpec((rank, rows), lambda i: (0, 0)),
            pl.BlockSpec((rows, depth), lambda i: (0, 0)),
            pl.BlockSpec((spread, rows), lambda i: (0, 0)),
            pl.BlockSpec((rows, hidden // steps), lambda i: (0, i)),
            own,
            own,
        ],
        out_specs=[by_rows, by_columns, own, own],
        compiler_params=pltpu.CompilerParams(vmem_limit_bytes=67043328),
    )(code_grad, slot_of, tok, code_wide_t, up_grad, layer, inward)


def on_device(
    tokens,
    output_gradient,
    gate_up_weight,
    down_weight,
    adapter_input_factor,
    adapter_output_factor,
    request_token_rows,
    request_adapter,
    adapter_table_row,
):
    rank = adapter_input_factor.shape[1]
    hidden_portion, width = down_weight.shape
    in_rows = adapter_input_factor.shape[0]
    out_rows = adapter_output_factor.shape[0]
    out_table = adapter_output_factor.reshape(out_rows * rank, hidden_portion)
    token_cols, code_wide_t, code_grad, slot_of, layer_output, input_gradient, up_grad = layer_call(
        request_token_rows.T, request_adapter.T, adapter_table_row, tokens, output_gradient,
        gate_up_weight, down_weight, adapter_input_factor, out_table, ("dp", "tensor"),
    )
    adapter_input_gradient, adapter_output_gradient, layer_output, input_gradient = adapter_call(
        code_grad, slot_of, in_rows, "tensor", token_cols, code_wide_t, up_grad,
        layer_output, input_gradient,
    )
    adapter_input_gradient = adapter_input_gradient.reshape(in_rows, rank, width)
    adapter_output_gradient = adapter_output_gradient.reshape(out_rows, rank, hidden_portion)
    return (layer_output, input_gradient, adapter_input_gradient, adapter_output_gradient)


def solution(mesh):
    in_specs = (
        P("dp", None),
        P("dp", None),
        P("dp", None, "tensor"),
        P("tensor", "dp"),
        P("tensor", None, "dp"),
        P("dp", None, "tensor"),
        P(),
        P(),
        P(),
    )
    out_specs = (
        P("tensor", "dp"),
        P("tensor", "dp"),
        P("tensor", None, "dp"),
        P("dp", None, "tensor"),
    )
    return jax.shard_map(
        on_device, mesh=mesh, in_specs=in_specs, out_specs=out_specs, check_vma=False
    )
```
